256 devices in a mesh: rows: 64 (over y, z, core), rhs: 4 (over x).
Axes of the slice: x: 4, y: 4, z: 8, core: 2. Of those that a mesh axis runs over, the one named last changes fastest.
Arguments:
- factor_left: bfloat16 [8192, 128, 128], P(('rows', 'rhs')), may hold values from -0.5 to 0.5
- factor_right: bfloat16 [8192, 128, 128], P(('rows', 'rhs')), may hold values from -0.5 to 0.5
- state_diag: float32 [8192, 128], P(('rows', 'rhs')), may hold values from 0.02 to 0.2
- owner: int32 [8192, 1], P(('rows', 'rhs')), may hold values from 0 to 63; in each aligned block of 32 rows (0 to 31, 32 to 63, ...) at most 2 rows name the same one
- col_local: int32 [8192], P(('rows', 'rhs')), may hold values from 0 to 15
- row_shift: int32 [8192], P(('rows', 'rhs')), may hold values from 0 to 2
- row_local: int32 [8192], P(('rows', 'rhs')), may hold values from 0 to 15
- rhs_in: float32 [1024, 256, 128], P('rows', 'rhs'), may hold values from -6 to 6
- low_bound: float32 [1], replicated, may hold values from 0.55 to 0.7
- high_bound: float32 [1], replicated, may hold values from 1.3 to 1.5
Outputs:
- adjoint: float32 [1024, 256, 128], P('rows', 'rhs')
- residual: float32 [1024, 256, 128], P('rows', 'rhs')
The draws below stay inside these ranges and needn't reach their ends.
Inputs may be any that keep to these rules, and one draw needn't show every extreme that they name: Among the 32 blocks of one device no owner is named more than 2 times, and every draw has a device that names some owner 2 times.
All inputs are finite; a program needn't handle non-finite values.
Results may differ from the reference program's by a relative error of at most 0.0082.
Values may be sent and summed in bfloat16 or wider, within the bound.
No kernel may reach another device: no remote copies, remote signals or barrier semaphores. Data moves between devices by JAX's collectives and lax.ppermute only.
A program may use at most 128 MiB of HBM per device.

```python
import math
import jax
import jax.numpy as jnp
import numpy as np
from jax import lax

BS = 128
RHS = 256
ITERS = 4
ROWS_DEV = 16
SLOT_DEV = 32
CAP = 2
NB = 1024
NNZ = 8192
N_ROWS = 64


def set_ends(result, stream_key, smallest, largest):
    extent = result.shape
    spot = [jax.random.randint(jax.random.fold_in(stream_key, axis), (), 0, extent[axis]) for axis in range(len(extent))]
    result = result.at[tuple(spot)].set(smallest)
    longest = extent.index(max(extent))
    spot[longest] = (spot[longest] + 1) % extent[longest]
    return result.at[tuple(spot)].set(largest)


def shard_levels(rng, extent, shards, least, top_value):
    gain = 1.0
    for dim, blocks in shards:
        heights = jax.random.uniform(jax.random.fold_in(jax.random.fold_in(rng, 6), dim), (blocks,), jnp.float32, least / len(shards), top_value / len(shards))
        gain = gain * jnp.repeat(jnp.exp(heights), extent[dim] // blocks).reshape((-1,) + (1,) * (len(extent) - 1 - dim))
    return gain


def routed_block(own_key, own, number, rows, amount, top, most, slope):
    sequence = jax.random.permutation(own_key, amount)
    heavy_load, common = load_shares(amount, rows * top, most, slope, True), load_shares(amount, rows * top, most, slope, False)
    places = jnp.arange(amount)

    def named(lengths, offset_by):
        used = int((lengths > 0).sum())
        fixed = max(1, used // 4)
        shifted = fixed + (places - fixed + offset_by * (used - fixed)) % max(1, amount - fixed)
        return jnp.zeros((amount,), jnp.int32).at[sequence[jnp.where(places < fixed, places, shifted)]].set(jnp.asarray(lengths, jnp.int32))

    lengths = jnp.where(number % 4 == 0, named(heavy_load, number // 4), named(common, number - number // 4 - 1))
    mixed = jax.random.permutation(jax.random.fold_in(own, 3), amount)
    giver, taker = mixed[0:amount // 2 * 2:2], mixed[1:amount // 2 * 2:2]
    room = jnp.minimum(lengths[giver] - 1, most - lengths[taker]) // 2
    room = jnp.where((giver == sequence[0]) | (taker == sequence[0]) | (lengths[taker] == 0), 0, jnp.maximum(room, 0))
    shifted = jax.random.randint(jax.random.fold_in(own, 4), (amount // 2,), 0, 1 << 20) % (room + 1)
    lengths = lengths.at[giver].add(-shifted).at[taker].add(shifted)
    labels = jnp.searchsorted(jnp.cumsum(lengths), jnp.arange(rows * top), side="right").astype(jnp.int32)
    table = labels.reshape(top, rows).T
    table = table[jax.random.permutation(jax.random.fold_in(own, 1), rows)]
    offset_by = jax.random.randint(jax.random.fold_in(own, 2), (rows, 1), 0, top)
    return jnp.take_along_axis(table, (jnp.arange(top)[None, :] + offset_by) % top, axis=1)


def load_shares(number_of, total, most, skew, full):
    weights = [(1 << 20) // math.isqrt(rank ** skew) + 1 for rank in range(1, number_of + 1)]
    largest = most if full else min(most, max(-(-total // number_of), total * weights[0] // sum(weights)))
    least = 1 if total - largest >= number_of - 1 else 0
    holding, rest = [largest] + [least] * (number_of - 1), total - largest - least * (number_of - 1)
    while rest > 0:
        free = [i for i in range(1, number_of) if holding[i] < largest] or [i for i in range(1, number_of) if holding[i] < most]
        whole, budget = sum([weights[i] for i in free]), rest
        for i in free:
            extra = min(most - holding[i], max(1, budget * weights[i] // whole), rest)
            holding[i] = holding[i] + extra
            rest = rest - extra
    return np.array(holding)


def scatter_about(rng, extent, scale, most, shards=(), held_as=jnp.bfloat16):
    factor_of = shard_levels(rng, extent, shards, -0.22, 0.18) if shards else 1.0
    array = jax.random.normal(rng, extent, jnp.float32) * scale * factor_of
    return jnp.minimum(jnp.maximum(array, -most), most).astype(held_as)


def setup_inputs(seed: int = 0) -> dict:
    splits = jax.random.split(jax.random.key(seed), 11)
    factor_left = scatter_about(splits[0], (NNZ, BS, BS), BS ** -0.5, 0.5, ((0, 256),))
    factor_right = scatter_about(splits[1], (NNZ, BS, BS), BS ** -0.5, 0.5, ((0, 256),))
    state_diag = jnp.clip(jnp.exp(math.log(0.2) - 2.3025851 * jax.random.uniform(splits[2], (NNZ, BS), jnp.float32) ** shard_levels(splits[2], (NNZ, BS), ((0, 256),), -0.2, 0.2)), 0.02, 0.2)
    owner_keys = jax.random.split(jax.random.fold_in(splits[3], 1), NNZ // SLOT_DEV)
    owner_turns = jax.random.permutation(jax.random.fold_in(splits[3], 3), NNZ // SLOT_DEV)
    owner = jax.vmap(lambda own, number: routed_block(jax.random.fold_in(splits[3], 2), own, number, SLOT_DEV, N_ROWS, 1, CAP, 2))(owner_keys, owner_turns).reshape((NNZ, 1))
    col_local = set_ends(jax.random.randint(splits[4], (NNZ,), 0, ROWS_DEV), jax.random.fold_in(splits[4], 1), 0, ROWS_DEV - 1).astype(jnp.int32)
    row_shift = set_ends(jax.random.randint(splits[5], (NNZ,), 0, 3), jax.random.fold_in(splits[5], 1), 0, 2).astype(jnp.int32)
    row_local = set_ends(jax.random.randint(splits[6], (NNZ,), 0, ROWS_DEV), jax.random.fold_in(splits[6], 1), 0, ROWS_DEV - 1).astype(jnp.int32)
    rhs_in = scatter_about(splits[7], (NB, RHS, BS), 1.0, 6.0, ((0, 64), (1, 4)), jnp.float32)
    low_bound = jnp.clip(jax.random.uniform(splits[8], (1,), jnp.float32, 0.55, 0.7), 0.55, 0.7)
    high_bound = jnp.clip(jax.random.uniform(splits[9], (1,), jnp.float32, 1.3, 1.5), 1.3, 1.5)
    return dict(factor_left=factor_left, factor_right=factor_right, state_diag=state_diag, owner=owner, col_local=col_local, row_shift=row_shift, row_local=row_local, rhs_in=rhs_in, low_bound=low_bound, high_bound=high_bound)


def form_group(items):
    left, right, diag = items
    scaled = (diag[:, :, None] * right.astype(jnp.float32)).astype(jnp.bfloat16)
    scaled = lax.optimization_barrier(scaled)
    product = jnp.einsum('kam,kmb->kab', left.astype(jnp.float32), scaled.astype(jnp.float32), precision=lax.Precision.HIGHEST)
    return product.astype(jnp.bfloat16)


def reference(factor_left, factor_right, state_diag, owner, col_local, row_shift, row_local, rhs_in, low_bound, high_bound):
    group = math.gcd(NNZ, 256)
    count = NNZ // group
    blocks = lax.map(form_group, (factor_left.reshape(count, group, BS, BS), factor_right.reshape(count, group, BS, BS), state_diag.reshape(count, group, BS)))
    dest = owner[:, 0].astype(jnp.int32)
    col_index = (dest * ROWS_DEV + col_local).astype(jnp.int32)
    row_index = ((dest + row_shift - 1) * ROWS_DEV + row_local) % NB
    row_index = row_index.astype(jnp.int32)
    col_groups = col_index.reshape(count, group)
    row_groups = row_index.reshape(count, group)

    def apply_operator(field):
        rounded = lax.optimization_barrier(field.astype(jnp.bfloat16)).astype(jnp.float32)

        def add_group(total, items):
            blk, rows_here, cols_here = items
            picked = rounded[rows_here]
            product = jnp.einsum('khb,kbc->khc', picked, blk.astype(jnp.float32), precision=lax.Precision.HIGHEST)
            return total.at[cols_here].add(product), None

        total, _ = lax.scan(add_group, jnp.zeros_like(field), (blocks, row_groups, col_groups))
        return field - total

    low = low_bound[0]
    high = high_bound[0]
    theta = (high + low) / 2.0
    delta = (high - low) / 2.0
    sigma = theta / delta
    rho = 1.0 / sigma
    adjoint = jnp.zeros_like(rhs_in)
    residual = rhs_in
    direction = residual / theta
    for sweep in range(ITERS):
        adjoint = adjoint + direction
        residual = residual - apply_operator(direction)
        if sweep + 1 < ITERS:
            rho_next = 1.0 / (2.0 * sigma - rho)
            direction = rho_next * rho * direction + (2.0 * rho_next / delta) * residual
            rho = rho_next
    return adjoint, residual
```

```python
import functools

import jax
import jax.numpy as jnp
from jax import lax
from jax.experimental import pallas as pl
from jax.experimental.pallas import tpu as pltpu
from jax.sharding import PartitionSpec as P

ITERS = 4


def form_kernel(owner, place, left, right, diag, out0, out1, held, sems):
    slots = left.shape[0]
    columns = diag[...].T

    def target(k, out):
        return pltpu.make_async_copy(held.at[k], out.at[owner[k]], sems.at[k])

    for k in range(slots):
        scaled = (columns[:, k : k + 1] * right[k].astype(jnp.float32)).astype(jnp.bfloat16)
        held[k] = jnp.dot(left[k], scaled, preferred_element_type=jnp.float32).astype(jnp.bfloat16)

        @pl.when(place[k] == 0)
        def _():
            target(k, out0).start()

        @pl.when(place[k] != 0)
        def _():
            target(k, out1).start()

    for k in range(slots):
        target(k, out0).wait()


def form_blocks(left, right, diag, owner, place, peers):
    slots, width = diag.shape
    shape = jax.ShapeDtypeStruct((peers, width, width), jnp.bfloat16)
    return pl.pallas_call(
        form_kernel,
        out_shape=(shape, shape),
        grid_spec=pltpu.PrefetchScalarGridSpec(
            num_scalar_prefetch=2,
            in_specs=[pl.BlockSpec(memory_space=pltpu.VMEM)] * 3,
            out_specs=[pl.BlockSpec(memory_space=pl.ANY)] * 2,
            scratch_shapes=[
                pltpu.VMEM((slots, width, width), jnp.bfloat16),
                pltpu.SemaphoreType.DMA((slots,)),
            ],
        ),
        name="form_blocks",
    )(owner, place, left, right, diag)


def pack_kernel(order, count, got, first, second, sems):
    half = first.shape[0]
    total = count[0]

    def lower(j, carry):
        pltpu.make_async_copy(got.at[order[j]], first.at[j], sems.at[j]).start()
        return carry

    def upper(j, carry):
        pltpu.make_async_copy(got.at[order[j]], second.at[j - half], sems.at[j]).start()
        return carry

    def finish(j, carry):
        pltpu.make_async_copy(got.at[0], first.at[0], sems.at[j]).wait()
        return carry

    lax.fori_loop(0, jnp.minimum(total, half), lower, 0)
    lax.fori_loop(half, jnp.maximum(total, half), upper, 0)
    lax.fori_loop(0, total, finish, 0)


def pack_blocks(got, order, count):
    peers, width, _ = got.shape
    shape = jax.ShapeDtypeStruct((peers // 2, width, width), jnp.bfloat16)
    return pl.pallas_call(
        pack_kernel,
        out_shape=(shape, shape),
        grid_spec=pltpu.PrefetchScalarGridSpec(
            num_scalar_prefetch=2,
            in_specs=[pl.BlockSpec(memory_space=pl.ANY)],
            out_specs=[pl.BlockSpec(memory_space=pl.ANY)] * 2,
            scratch_shapes=[pltpu.SemaphoreType.DMA((peers,))],
        ),
        name="pack_blocks",
    )(order, count, got)


def apply_blocks(parts, chunk, counts, codes, ext, acc, held, sems):
    half = parts[0].shape[0]
    steps = half // chunk
    rows = acc.shape[0] - 1
    reads = ext.shape[0]
    for a, part in enumerate(parts):
        for c in range(steps):

            @pl.when(counts[a] > c * chunk)
            def _():
                pltpu.make_async_copy(
                    part.at[pl.ds(c * chunk, chunk)],
                    held.at[pl.ds(a * half + c * chunk, chunk)],
                    sems.at[a * steps + c],
                ).start()

    def part_body(a, carry):
        def chunk_body(c, inner):
            base = a * half + c * chunk
            pltpu.make_async_copy(
                parts[0].at[pl.ds(0, chunk)], held.at[pl.ds(base, chunk)], sems.at[a * steps + c]
            ).wait()
            products, cols = [], []
            for j in range(chunk):
                code = codes[base + j]
                filled = code > 0
                value = jnp.where(filled, code - 1, rows * reads)
                col = lax.div(value, reads)
                read = value - col * reads
                cols.append(col)
                products.append(
                    jnp.dot(ext[read], held[base + j], preferred_element_type=jnp.float32)
                )
            for col, product in zip(cols, products):
                acc[col] += product
            return inner

        return lax.fori_loop(0, lax.div(counts[a] + chunk - 1, chunk), chunk_body, carry)

    lax.fori_loop(0, len(parts), part_body, 0)


def sweep_kernel(num_parts, chunk, has_acc, last, final, *refs):
    counts, codes, coef = refs[:3]
    refs = refs[3:]
    parts, refs = refs[:num_parts], refs[num_parts:]
    low, mid, high = refs[:3]
    refs = refs[3:]
    if has_acc:
        acc_in, refs = refs[0], refs[1:]
    if last:
        adjoint, residual, direction = refs[:3]
        refs = refs[3:]
        outs, refs = (refs[:2], refs[2:]) if final else (refs[:4], refs[4:])
    else:
        outs, refs = refs[:1], refs[1:]
    ext, acc, held, sems = refs
    rows = mid.shape[0]
    ext[pl.ds(0, rows)] = low[...]
    ext[pl.ds(rows, rows)] = mid[...]
    ext[pl.ds(2 * rows, rows)] = high[...]
    acc[pl.ds(0, rows)] = acc_in[...] if has_acc else jnp.zeros(mid.shape, jnp.float32)
    acc[rows] = jnp.zeros(mid.shape[1:], jnp.float32)
    apply_blocks(parts, chunk, counts, codes, ext, acc, held, sems)
    if not last:
        outs[0][...] = acc[pl.ds(0, rows)]
        return
    step = direction[...]
    left = residual[...] - (step - acc[pl.ds(0, rows)])
    if final:
        outs[0][...] = adjoint[...]
        outs[1][...] = left
        return
    step = coef[0] * step + coef[1] * left
    outs[0][...] = adjoint[...] + step
    outs[1][...] = left
    outs[2][...] = step
    outs[3][...] = step.astype(jnp.bfloat16)


def sweep(parts, counts, codes, coef, fields, acc_in=None, state=None, final=False):
    half, width, _ = parts[0].shape
    chunk = min(8, half)
    rows, columns, _ = fields[1].shape
    last = state is not None
    wide = jax.ShapeDtypeStruct((rows, columns, width), jnp.float32)
    if not last:
        outs = (wide,)
    elif final:
        outs = (wide, wide)
    else:
        outs = (wide, wide, wide, jax.ShapeDtypeStruct(wide.shape, jnp.bfloat16))
    extra = list(fields) + ([acc_in] if acc_in is not None else []) + list(state or ())
    aliases = {}
    return pl.pallas_call(
        functools.partial(sweep_kernel, len(parts), chunk, acc_in is not None, last, final),
        out_shape=outs,
        in_specs=[pl.BlockSpec(memory_space=pltpu.SMEM)] * 3
        + [pl.BlockSpec(memory_space=pl.ANY)] * len(parts)
        + [pl.BlockSpec(memory_space=pltpu.VMEM)] * len(extra),
        out_specs=[pl.BlockSpec(memory_space=pltpu.VMEM)] * len(outs),
        scratch_shapes=[
            pltpu.VMEM((3 * rows, columns, width), jnp.bfloat16),
            pltpu.VMEM((rows + 1, columns, width), jnp.float32),
            pltpu.VMEM((len(parts) * half, width, width), jnp.bfloat16),
            pltpu.SemaphoreType.DMA((len(parts) * (half // chunk),)),
        ],
        input_output_aliases=aliases,
        compiler_params=pltpu.CompilerParams(vmem_limit_bytes=40 * 2**20),
        name="sweep",
    )(counts, codes, coef, *parts, *extra)


def ring(count, shift):
    return [(i, (i + shift) % count) for i in range(count)]


def spread(pair, count):
    up, down = ring(count, 1), ring(count, -1)
    first, second = pair
    up_first = lax.ppermute(first, "rhs", up)
    down_second = lax.ppermute(second, "rhs", down)
    far_first = lax.ppermute(up_first, "rhs", up)
    far_second = lax.ppermute(down_second, "rhs", down)
    up_second = lax.ppermute(second, "rhs", up)
    down_first = lax.ppermute(first, "rhs", down)
    return [first, second, up_first, up_second, down_first, down_second, far_first, far_second]


def neighbours(rounded):
    count = lax.axis_size("rows")
    return (
        lax.ppermute(rounded, "rows", ring(count, 1)),
        rounded,
        lax.ppermute(rounded, "rows", ring(count, -1)),
    )


def local(
    factor_left,
    factor_right,
    state_diag,
    owner,
    col_local,
    row_shift,
    row_local,
    rhs_in,
    low_bound,
    high_bound,
):
    peers = lax.axis_size("rows")
    across = lax.axis_size("rhs")
    slots = owner.shape[0]
    local_rows = rhs_in.shape[0]
    reads = 3 * local_rows
    dest = owner[:, 0]
    order = jnp.arange(slots)
    earlier = (dest[:, None] == dest[None, :]) & (order[None, :] < order[:, None])
    place = jnp.sum(earlier.astype(jnp.int32), axis=1)
    code = col_local * reads + row_shift * local_rows + row_local + 1
    spot = dest * 2 + place
    send_codes = jnp.sum(
        jnp.where(jnp.arange(2 * peers)[:, None] == spot[None, :], code[None, :], 0), axis=1
    )
    got_codes = lax.all_to_all(
        send_codes.reshape(peers, 2), "rows", split_axis=0, concat_axis=0, tiled=True
    ).T
    number = jnp.arange(peers)
    key = jnp.where(got_codes > 0, got_codes, jnp.int32(1 << 20))
    ahead = (key[:, None, :] < key[:, :, None]) | (
        (key[:, None, :] == key[:, :, None]) & (number[None, None, :] < number[None, :, None])
    )
    rank = jnp.sum(ahead.astype(jnp.int32), axis=2)
    chosen = rank[:, None, :] == number[None, :, None]
    source = jnp.sum(jnp.where(chosen, number[None, None, :], 0), axis=2)
    sorted_codes = jnp.sum(jnp.where(chosen, got_codes[:, None, :], 0), axis=2)
    count = jnp.sum((got_codes > 0).astype(jnp.int32), axis=1)

    up = lax.ppermute(sorted_codes, "rhs", ring(across, 1))
    down = lax.ppermute(sorted_codes, "rhs", ring(across, -1))
    far = lax.ppermute(sorted_codes, "rhs", ring(across, 2))
    all_codes = jnp.stack([sorted_codes, up, down, far], axis=1).reshape(2, 4, 2, peers // 2)
    all_counts = jnp.sum((all_codes > 0).astype(jnp.int32), axis=3).reshape(2, 8)
    all_codes = all_codes.reshape(2, 4 * peers)

    sent0, sent1 = form_blocks(factor_left, factor_right, state_diag, dest, place, peers)
    got0 = lax.all_to_all(sent0, "rows", split_axis=0, concat_axis=0, tiled=True)
    got1 = lax.all_to_all(sent1, "rows", split_axis=0, concat_axis=0, tiled=True)
    parts0 = spread(pack_blocks(got0, source[0], count[:1]), across)
    parts1 = spread(pack_blocks(got1, source[1], count[1:]), across)

    low = low_bound[0]
    high = high_bound[0]
    theta = (high + low) / 2.0
    delta = (high - low) / 2.0
    sigma = theta / delta
    rho = 1.0 / sigma
    residual = rhs_in
    direction = residual / theta
    adjoint = direction
    fields = neighbours(direction.astype(jnp.bfloat16))
    for number in range(ITERS):
        rho_next = 1.0 / (2.0 * sigma - rho)
        coef = jnp.stack([rho_next * rho, 2.0 * rho_next / delta])
        rho = rho_next
        state = (adjoint, residual, direction)
        final = number + 1 == ITERS
        if number == 0:
            (acc,) = sweep(parts0, all_counts[0], all_codes[0], coef, fields)
            out = sweep(parts1, all_counts[1], all_codes[1], coef, fields, acc, state)
        else:
            out = sweep(
                parts0 + parts1,
                all_counts.reshape(16),
                all_codes.reshape(8 * peers),
                coef,
                fields,
                None,
                state,
                final,
            )
        if final:
            return out
        adjoint, residual, direction, rounded = out
        fields = neighbours(rounded)


def solution(mesh):
    placed = (
        P(("rows", "rhs"), None, None),
        P(("rows", "rhs"), None, None),
        P(("rows", "rhs"), None),
        P(("rows", "rhs"), None),
        P(("rows", "rhs")),
        P(("rows", "rhs")),
        P(("rows", "rhs")),
        P("rows", "rhs", None),
        P(),
        P(),
    )
    return jax.shard_map(
        local,
        mesh=mesh,
        in_specs=placed,
        out_specs=(P("rows", "rhs", None), P("rows", "rhs", None)),
        check_vma=False,
    )
```

```python
import functools

import jax
import jax.numpy as jnp
from jax import lax
from jax.experimental import pallas as pl
from jax.experimental.pallas import tpu as pltpu
from jax.sharding import PartitionSpec as P

ITERS = 4
CHUNK = 16


def form_kernel(owner, place, left, right, diag, out0, out1, held, sems):
    slots = left.shape[0]
    columns = diag[...].T

    def target(k, out):
        return pltpu.make_async_copy(held.at[k], out.at[owner[k]], sems.at[k])

    for k in range(slots):
        scaled = (columns[:, k : k + 1] * right[k].astype(jnp.float32)).astype(jnp.bfloat16)
        held[k] = jnp.dot(left[k], scaled, preferred_element_type=jnp.float32).astype(jnp.bfloat16)

        @pl.when(place[k] == 0)
        def _():
            target(k, out0).start()

        @pl.when(place[k] != 0)
        def _():
            target(k, out1).start()

    for k in range(slots):
        target(k, out0).wait()


def form_blocks(left, right, diag, owner, place, peers):
    slots, width = diag.shape
    shape = jax.ShapeDtypeStruct((peers, width, width), jnp.bfloat16)
    return pl.pallas_call(
        form_kernel,
        out_shape=(shape, shape),
        grid_spec=pltpu.PrefetchScalarGridSpec(
            num_scalar_prefetch=2,
            in_specs=[pl.BlockSpec(memory_space=pltpu.VMEM)] * 3,
            out_specs=[pl.BlockSpec(memory_space=pltpu.HBM)] * 2,
            scratch_shapes=[
                pltpu.VMEM((slots, width, width), jnp.bfloat16),
                pltpu.SemaphoreType.DMA((slots,)),
            ],
        ),
        name="form_blocks",
    )(owner, place, left, right, diag)


def pack_kernel(order, count, got, first, second, sems):
    half = first.shape[0]
    total = count[0]

    def lower(j, carry):
        pltpu.make_async_copy(got.at[order[j]], first.at[j], sems.at[j]).start()
        return carry

    def upper(j, carry):
        pltpu.make_async_copy(got.at[order[j]], second.at[j - half], sems.at[j]).start()
        return carry

    def finish(j, carry):
        pltpu.make_async_copy(got.at[0], first.at[0], sems.at[j]).wait()
        return carry

    lax.fori_loop(0, jnp.minimum(total, half), lower, 0)
    lax.fori_loop(half, jnp.maximum(total, half), upper, 0)
    lax.fori_loop(0, total, finish, 0)


def pack_blocks(got, order, count):
    peers, width, _ = got.shape
    shape = jax.ShapeDtypeStruct((peers // 2, width, width), jnp.bfloat16)
    return pl.pallas_call(
        pack_kernel,
        out_shape=(shape, shape),
        grid_spec=pltpu.PrefetchScalarGridSpec(
            num_scalar_prefetch=2,
            in_specs=[pl.BlockSpec(memory_space=pltpu.VMEM)],
            out_specs=[pl.BlockSpec(memory_space=pltpu.HBM)] * 2,
            scratch_shapes=[pltpu.SemaphoreType.DMA((peers,))],
        ),
        name="pack_blocks",
    )(order, count, got)


def read_bits(rows):
    return (3 * rows - 1).bit_length()


def sweep_kernel(num_parts, chunk, has_acc, last, final, *refs):
    counts, codes, coef = refs[:3]
    refs = refs[3:]
    parts, refs = refs[:num_parts], refs[num_parts:]
    fields, refs = refs[:3], refs[3:]
    num_state = 3 * last + has_acc
    state, refs = refs[:num_state], refs[num_state:]
    num_outs = (2 if final else 4) if last else 1
    outs, refs = refs[:num_outs], refs[num_outs:]
    ext, acc, held, kept, rounded, sems, field_sems, state_sems, out_sems = refs
    rows = fields[1].shape[0]
    half = parts[0].shape[0]
    steps = half // chunk
    bits = read_bits(rows)
    field_copies = [
        pltpu.make_async_copy(field, ext.at[pl.ds(i * rows, rows)], field_sems.at[i])
        for i, field in enumerate(fields)
    ]
    for copy in field_copies:
        copy.start()
    for a, part in enumerate(parts):
        for c in range(steps):

            @pl.when(counts[a] > c * chunk)
            def _():
                pltpu.make_async_copy(
                    part.at[pl.ds(c * chunk, chunk)],
                    held.at[pl.ds(a * half + c * chunk, chunk)],
                    sems.at[a * steps + c],
                ).start()

    used = acc.at[pl.ds(1, rows)]
    state_copies = [
        pltpu.make_async_copy(array, kept.at[i], state_sems.at[i])
        for i, array in enumerate(state[: 3 * last])
    ]
    if has_acc:
        acc_copy = pltpu.make_async_copy(state[-1], used, state_sems.at[3])
        acc_copy.start()
    else:
        used[...] = jnp.zeros(used.shape, jnp.float32)
    acc[0] = jnp.zeros(acc.shape[1:], jnp.float32)
    for copy in state_copies:
        copy.start()
    for copy in field_copies:
        copy.wait()
    if has_acc:
        acc_copy.wait()

    def part_body(a, carry):
        def chunk_body(c, inner):
            base = a * half + c * chunk
            pltpu.make_async_copy(
                parts[0].at[pl.ds(0, chunk)], held.at[pl.ds(base, chunk)], sems.at[a * steps + c]
            ).wait()
            for j in range(chunk):
                code = codes[base + j]
                picked = ext[code & (2**bits - 1)]
                acc[code >> bits] += jnp.dot(
                    picked, held[base + j], preferred_element_type=jnp.float32
                )
            return inner

        return lax.fori_loop(0, lax.div(counts[a] + chunk - 1, chunk), chunk_body, carry)

    lax.fori_loop(0, num_parts, part_body, 0)

    if not last:
        results = [used]
    else:
        for copy in state_copies:
            copy.wait()
        adjoint, residual, direction = (kept.at[i] for i in range(3))
        step = direction[...]
        left = residual[...] - (step - used[...])
        residual[...] = left
        results = [adjoint, residual]
        if not final:
            step = coef[0] * step + coef[1] * left
            rounded[...] = step.astype(jnp.bfloat16)
            direction[...] = step
            adjoint[...] = adjoint[...] + step
            results = [rounded, adjoint, residual, direction]
    out_copies = [
        pltpu.make_async_copy(result, out, out_sems.at[i])
        for i, (result, out) in enumerate(zip(results, outs))
    ]
    for copy in out_copies:
        copy.start()
    for copy in out_copies:
        copy.wait()


def sweep(parts, counts, codes, coef, fields, acc_in=None, state=None, final=False):
    half, width, _ = parts[0].shape
    chunk = min(CHUNK, half)
    rows, columns, _ = fields[1].shape
    last = state is not None
    wide = jax.ShapeDtypeStruct((rows, columns, width), jnp.float32)
    if not last:
        outs = (wide,)
    elif final:
        outs = (wide, wide)
    else:
        outs = (jax.ShapeDtypeStruct(wide.shape, jnp.bfloat16), wide, wide, wide)
    extra = list(fields) + list(state or ()) + ([acc_in] if acc_in is not None else [])
    return pl.pallas_call(
        functools.partial(sweep_kernel, len(parts), chunk, acc_in is not None, last, final),
        out_shape=outs,
        in_specs=[pl.BlockSpec(memory_space=pltpu.SMEM)] * 3
        + [pl.BlockSpec(memory_space=pltpu.HBM)] * (len(parts) + len(extra)),
        out_specs=[pl.BlockSpec(memory_space=pltpu.HBM)] * len(outs),
        scratch_shapes=[
            pltpu.VMEM((3 * rows, columns, width), jnp.bfloat16),
            pltpu.VMEM((rows + 1, columns, width), jnp.float32),
            pltpu.VMEM((len(parts) * half, width, width), jnp.bfloat16),
            pltpu.VMEM((3, rows, columns, width), jnp.float32),
            pltpu.VMEM((rows, columns, width), jnp.bfloat16),
            pltpu.SemaphoreType.DMA((len(parts) * (half // chunk),)),
            pltpu.SemaphoreType.DMA((3,)),
            pltpu.SemaphoreType.DMA((4,)),
            pltpu.SemaphoreType.DMA((4,)),
        ],
        compiler_params=pltpu.CompilerParams(vmem_limit_bytes=60 * 2**20),
        name="sweep",
    )(counts, codes, coef, *parts, *extra)


def ring(count, shift):
    return [(i, (i + shift) % count) for i in range(count)]


def spread(pair, count):
    up, down = ring(count, 1), ring(count, -1)
    first, second = pair
    up_first = lax.ppermute(first, "rhs", up)
    down_second = lax.ppermute(second, "rhs", down)
    far_first = lax.ppermute(up_first, "rhs", up)
    far_second = lax.ppermute(down_second, "rhs", down)
    up_second = lax.ppermute(second, "rhs", up)
    down_first = lax.ppermute(first, "rhs", down)
    return [first, second, up_first, up_second, down_first, down_second, far_first, far_second]


def neighbours(rounded):
    count = lax.axis_size("rows")
    return (
        lax.ppermute(rounded, "rows", ring(count, 1)),
        rounded,
        lax.ppermute(rounded, "rows", ring(count, -1)),
    )


def local(
    factor_left,
    factor_right,
    state_diag,
    owner,
    col_local,
    row_shift,
    row_local,
    rhs_in,
    low_bound,
    high_bound,
):
    peers = lax.axis_size("rows")
    across = lax.axis_size("rhs")
    slots = owner.shape[0]
    local_rows = rhs_in.shape[0]
    bits = read_bits(local_rows)
    dest = owner[:, 0]
    order = jnp.arange(slots)
    earlier = (dest[:, None] == dest[None, :]) & (order[None, :] < order[:, None])
    place = jnp.sum(earlier.astype(jnp.int32), axis=1)
    code = ((col_local + 1) << bits) + row_shift * local_rows + row_local
    spot = dest * 2 + place
    send_codes = jnp.sum(
        jnp.where(jnp.arange(2 * peers)[:, None] == spot[None, :], code[None, :], 0), axis=1
    )
    with jax.named_scope("code_exchange"):
        got_codes = lax.all_to_all(
            send_codes.reshape(peers, 2), "rows", split_axis=0, concat_axis=0, tiled=True
        ).T
    number = jnp.arange(peers)
    key = jnp.where(got_codes > 0, got_codes, jnp.int32(1 << 20))
    ahead = (key[:, None, :] < key[:, :, None]) | (
        (key[:, None, :] == key[:, :, None]) & (number[None, None, :] < number[None, :, None])
    )
    rank = jnp.sum(ahead.astype(jnp.int32), axis=2)
    chosen = rank[:, None, :] == number[None, :, None]
    source = jnp.sum(jnp.where(chosen, number[None, None, :], 0), axis=2)
    sorted_codes = jnp.sum(jnp.where(chosen, got_codes[:, None, :], 0), axis=2)
    count = jnp.sum((got_codes > 0).astype(jnp.int32), axis=1)

    up = lax.ppermute(sorted_codes, "rhs", ring(across, 1))
    down = lax.ppermute(sorted_codes, "rhs", ring(across, -1))
    far = lax.ppermute(sorted_codes, "rhs", ring(across, 2))
    all_codes = jnp.stack([sorted_codes, up, down, far], axis=1).reshape(2, 4, 2, peers // 2)
    all_counts = jnp.sum((all_codes > 0).astype(jnp.int32), axis=3).reshape(2, 8)
    all_codes = all_codes.reshape(2, 4 * peers)

    sent0, sent1 = form_blocks(factor_left, factor_right, state_diag, dest, place, peers)
    with jax.named_scope("block_exchange"):
        got0 = lax.all_to_all(sent0, "rows", split_axis=0, concat_axis=0, tiled=True)
    got1 = lax.all_to_all(sent1, "rows", split_axis=0, concat_axis=0, tiled=True)
    parts0 = spread(pack_blocks(got0, source[0], count[:1]), across)
    parts1 = spread(pack_blocks(got1, source[1], count[1:]), across)

    low = low_bound[0]
    high = high_bound[0]
    theta = (high + low) / 2.0
    delta = (high - low) / 2.0
    sigma = theta / delta
    rho = 1.0 / sigma
    residual = rhs_in
    direction = residual / theta
    adjoint = direction
    fields = neighbours(direction.astype(jnp.bfloat16))
    for number in range(ITERS):
        rho_next = 1.0 / (2.0 * sigma - rho)
        coef = jnp.stack([rho_next * rho, 2.0 * rho_next / delta])
        rho = rho_next
        state = (adjoint, residual, direction)
        final = number + 1 == ITERS
        if number == 0:
            (acc,) = sweep(parts0, all_counts[0], all_codes[0], coef, fields)
            out = sweep(parts1, all_counts[1], all_codes[1], coef, fields, acc, state)
        else:
            out = sweep(
                parts0 + parts1,
                all_counts.reshape(16),
                all_codes.reshape(8 * peers),
                coef,
                fields,
                None,
                state,
                final,
            )
        if final:
            return out
        rounded, adjoint, residual, direction = out
        fields = neighbours(rounded)


def solution(mesh):
    placed = (
        P(("rows", "rhs"), None, None),
        P(("rows", "rhs"), None, None),
        P(("rows", "rhs"), None),
        P(("rows", "rhs"), None),
        P(("rows", "rhs")),
        P(("rows", "rhs")),
        P(("rows", "rhs")),
        P("rows", "rhs", None),
        P(),
        P(),
    )
    return jax.shard_map(
        local,
        mesh=mesh,
        in_specs=placed,
        out_specs=(P("rows", "rhs", None), P("rows", "rhs", None)),
        check_vma=False,
    )
```

```python
import functools

import jax
import jax.numpy as jnp
from jax import lax
from jax.experimental import pallas as pl
from jax.experimental.pallas import tpu as pltpu
from jax.sharding import PartitionSpec as P

ITERS = 4
CHUNK = 32


def form_kernel(owner, place, left, right, diag, out0, out1, held, sems):
    slots = left.shape[0]
    columns = diag[...].T

    def target(k, out):
        return pltpu.make_async_copy(held.at[k], out.at[owner[k]], sems.at[k])

    for k in range(slots):
        scaled = (columns[:, k : k + 1] * right[k].astype(jnp.float32)).astype(jnp.bfloat16)
        held[k] = jnp.dot(left[k], scaled, preferred_element_type=jnp.float32).astype(jnp.bfloat16)

        @pl.when(place[k] == 0)
        def _():
            target(k, out0).start()

        @pl.when(place[k] != 0)
        def _():
            target(k, out1).start()

    for k in range(slots):
        target(k, out0).wait()


def form_blocks(left, right, diag, owner, place, peers):
    slots, width = diag.shape
    shape = jax.ShapeDtypeStruct((peers, width, width), jnp.bfloat16)
    return pl.pallas_call(
        form_kernel,
        out_shape=(shape, shape),
        grid_spec=pltpu.PrefetchScalarGridSpec(
            num_scalar_prefetch=2,
            in_specs=[pl.BlockSpec(memory_space=pltpu.VMEM)] * 3,
            out_specs=[pl.BlockSpec(memory_space=pltpu.HBM)] * 2,
            scratch_shapes=[
                pltpu.VMEM((slots, width, width), jnp.bfloat16),
                pltpu.SemaphoreType.DMA((slots,)),
            ],
        ),
        name="form_blocks",
    )(owner, place, left, right, diag)


def pack_kernel(order, count, got, packed, sems):
    def begin(j, carry):
        pltpu.make_async_copy(got.at[order[j]], packed.at[j], sems.at[j]).start()
        return carry

    def finish(j, carry):
        pltpu.make_async_copy(got.at[0], packed.at[0], sems.at[j]).wait()
        return carry

    lax.fori_loop(0, count[0], begin, 0)
    lax.fori_loop(0, count[0], finish, 0)


def pack_blocks(got, order, count):
    peers, width, _ = got.shape
    return pl.pallas_call(
        pack_kernel,
        out_shape=jax.ShapeDtypeStruct((peers, width, width), jnp.bfloat16),
        grid_spec=pltpu.PrefetchScalarGridSpec(
            num_scalar_prefetch=2,
            in_specs=[pl.BlockSpec(memory_space=pltpu.VMEM)],
            out_specs=pl.BlockSpec(memory_space=pltpu.HBM),
            scratch_shapes=[pltpu.SemaphoreType.DMA((peers,))],
        ),
        name="pack_blocks",
    )(order, count, got)


def read_bits(rows):
    return (3 * rows - 1).bit_length()


def sweep_kernel(num_parts, half, chunk, has_acc, last, final, *refs):
    counts, codes, coef = refs[:3]
    refs = refs[3:]
    parts, refs = refs[:num_parts], refs[num_parts:]
    fields, refs = refs[:3], refs[3:]
    num_state = 3 * last + has_acc
    state, refs = refs[:num_state], refs[num_state:]
    num_outs = (2 if final else 4) if last else 1
    outs, refs = refs[:num_outs], refs[num_outs:]
    ext, acc, held, kept, rounded, sems, field_sems, state_sems, out_sems = refs
    rows = fields[1].shape[0]
    steps = half // chunk
    halves = [(part, i) for part in parts for i in range(0, part.shape[0], half)]
    bits = read_bits(rows)
    field_copies = [
        pltpu.make_async_copy(field, ext.at[pl.ds(i * rows, rows)], field_sems.at[i])
        for i, field in enumerate(fields)
    ]
    for copy in field_copies:
        copy.start()
    for a, (part, first) in enumerate(halves):
        for c in range(steps):

            @pl.when(counts[a] > c * chunk)
            def _():
                pltpu.make_async_copy(
                    part.at[pl.ds(first + c * chunk, chunk)],
                    held.at[pl.ds(a * half + c * chunk, chunk)],
                    sems.at[a * steps + c],
                ).start()

    used = acc.at[pl.ds(1, rows)]
    state_copies = [
        pltpu.make_async_copy(array, kept.at[i], state_sems.at[i])
        for i, array in enumerate(state[: 3 * last])
    ]
    if has_acc:
        acc_copy = pltpu.make_async_copy(state[-1], used, state_sems.at[3])
        acc_copy.start()
    else:
        used[...] = jnp.zeros(used.shape, jnp.float32)
    acc[0] = jnp.zeros(acc.shape[1:], jnp.float32)
    for copy in state_copies:
        copy.start()
    for copy in field_copies:
        copy.wait()
    if has_acc:
        acc_copy.wait()

    def part_body(a, carry):
        def chunk_body(c, inner):
            base = a * half + c * chunk
            pltpu.make_async_copy(
                parts[0].at[pl.ds(0, chunk)], held.at[pl.ds(base, chunk)], sems.at[a * steps + c]
            ).wait()
            for j in range(chunk):
                code = codes[base + j]
                picked = ext[code & (2**bits - 1)]
                acc[code >> bits] += jnp.dot(
                    picked, held[base + j], preferred_element_type=jnp.float32
                )
            return inner

        return lax.fori_loop(0, lax.div(counts[a] + chunk - 1, chunk), chunk_body, carry)

    lax.fori_loop(0, len(halves), part_body, 0)

    if not last:
        results = [used]
    else:
        for copy in state_copies:
            copy.wait()
        adjoint, residual, direction = (kept.at[i] for i in range(3))
        step = direction[...]
        left = residual[...] - (step - used[...])
        residual[...] = left
        results = [adjoint, residual]
        if not final:
            step = coef[0] * step + coef[1] * left
            rounded[...] = step.astype(jnp.bfloat16)
            direction[...] = step
            adjoint[...] = adjoint[...] + step
            results = [rounded, adjoint, residual, direction]
    out_copies = [
        pltpu.make_async_copy(result, out, out_sems.at[i])
        for i, (result, out) in enumerate(zip(results, outs))
    ]
    for copy in out_copies:
        copy.start()
    for copy in out_copies:
        copy.wait()


def sweep(parts, counts, codes, coef, fields, acc_in=None, state=None, final=False):
    half, width = parts[-1].shape[:2]
    chunk = min(CHUNK, half)
    held = sum(part.shape[0] for part in parts)
    rows, columns, _ = fields[1].shape
    last = state is not None
    wide = jax.ShapeDtypeStruct((rows, columns, width), jnp.float32)
    if not last:
        outs = (wide,)
    elif final:
        outs = (wide, wide)
    else:
        outs = (jax.ShapeDtypeStruct(wide.shape, jnp.bfloat16), wide, wide, wide)
    extra = list(fields) + list(state or ()) + ([acc_in] if acc_in is not None else [])
    return pl.pallas_call(
        functools.partial(sweep_kernel, len(parts), half, chunk, acc_in is not None, last, final),
        out_shape=outs,
        in_specs=[pl.BlockSpec(memory_space=pltpu.SMEM)] * 3
        + [pl.BlockSpec(memory_space=pltpu.HBM)] * (len(parts) + len(extra)),
        out_specs=[pl.BlockSpec(memory_space=pltpu.HBM)] * len(outs),
        scratch_shapes=[
            pltpu.VMEM((3 * rows, columns, width), jnp.bfloat16),
            pltpu.VMEM((rows + 1, columns, width), jnp.float32),
            pltpu.VMEM((held, width, width), jnp.bfloat16),
            pltpu.VMEM((3, rows, columns, width), jnp.float32),
            pltpu.VMEM((rows, columns, width), jnp.bfloat16),
            pltpu.SemaphoreType.DMA((held // chunk,)),
            pltpu.SemaphoreType.DMA((3,)),
            pltpu.SemaphoreType.DMA((4,)),
            pltpu.SemaphoreType.DMA((4,)),
        ],
        compiler_params=pltpu.CompilerParams(vmem_limit_bytes=60 * 2**20),
        name="sweep",
    )(counts, codes, coef, *parts, *extra)


def ring(count, shift):
    return [(i, (i + shift) % count) for i in range(count)]


def near(packed):
    count = lax.axis_size("rhs")
    return (
        lax.ppermute(packed, "rhs", ring(count, 1)),
        lax.ppermute(packed, "rhs", ring(count, -1)),
    )


def far(above, below):
    count = lax.axis_size("rhs")
    half = above.shape[0] // 2
    return (
        lax.ppermute(above[:half], "rhs", ring(count, 1)),
        lax.ppermute(below[half:], "rhs", ring(count, -1)),
    )


def neighbours(rounded):
    count = lax.axis_size("rows")
    return (
        lax.ppermute(rounded, "rows", ring(count, 1)),
        rounded,
        lax.ppermute(rounded, "rows", ring(count, -1)),
    )


def local(
    factor_left,
    factor_right,
    state_diag,
    owner,
    col_local,
    row_shift,
    row_local,
    rhs_in,
    low_bound,
    high_bound,
):
    peers = lax.axis_size("rows")
    across = lax.axis_size("rhs")
    slots = owner.shape[0]
    local_rows = rhs_in.shape[0]
    bits = read_bits(local_rows)
    dest = owner[:, 0]
    order = jnp.arange(slots)
    earlier = (dest[:, None] == dest[None, :]) & (order[None, :] < order[:, None])
    place = jnp.sum(earlier.astype(jnp.int32), axis=1)
    code = ((col_local + 1) << bits) + row_shift * local_rows + row_local
    spot = dest * 2 + place
    send_codes = jnp.sum(
        jnp.where(jnp.arange(2 * peers)[:, None] == spot[None, :], code[None, :], 0), axis=1
    )
    with jax.named_scope("code_exchange"):
        got_codes = lax.all_to_all(
            send_codes.reshape(peers, 2), "rows", split_axis=0, concat_axis=0, tiled=True
        ).T
    number = jnp.arange(peers)
    key = jnp.where(got_codes > 0, got_codes, jnp.int32(1 << 20))
    ahead = (key[:, None, :] < key[:, :, None]) | (
        (key[:, None, :] == key[:, :, None]) & (number[None, None, :] < number[None, :, None])
    )
    rank = jnp.sum(ahead.astype(jnp.int32), axis=2)
    chosen = rank[:, None, :] == number[None, :, None]
    source = jnp.sum(jnp.where(chosen, number[None, None, :], 0), axis=2)
    sorted_codes = jnp.sum(jnp.where(chosen, got_codes[:, None, :], 0), axis=2)
    count = jnp.sum((got_codes > 0).astype(jnp.int32), axis=1)

    up = lax.ppermute(sorted_codes, "rhs", ring(across, 1))
    down = lax.ppermute(sorted_codes, "rhs", ring(across, -1))
    far_codes = lax.ppermute(sorted_codes, "rhs", ring(across, 2))
    all_codes = jnp.stack([sorted_codes, up, down, far_codes], axis=1)
    all_codes = all_codes.reshape(2, 4, 2, peers // 2)
    all_counts = jnp.sum((all_codes > 0).astype(jnp.int32), axis=3).reshape(2, 8)
    all_codes = all_codes.reshape(2, 4 * peers)
    tables = (
        source[0],
        source[1],
        count[:1],
        count[1:],
        all_counts[0],
        all_counts[1],
        all_counts.reshape(16),
        all_codes[0],
        all_codes[1],
        all_codes.reshape(8 * peers),
    )

    sent0, sent1 = form_blocks(factor_left, factor_right, state_diag, dest, place, peers)
    got0 = lax.all_to_all(sent0, "rows", split_axis=0, concat_axis=0, tiled=True)
    got0, *tables = lax.optimization_barrier((got0, *tables))
    order0, order1, number0, number1, counts0, counts1, counts, codes0, codes1, codes = tables
    packed0 = pack_blocks(got0, order0, number0)
    near0 = near(packed0)
    got1 = lax.all_to_all(sent1, "rows", split_axis=0, concat_axis=0, tiled=True)
    packed1 = pack_blocks(got1, order1, number1)

    low = low_bound[0]
    high = high_bound[0]
    theta = (high + low) / 2.0
    delta = (high - low) / 2.0
    sigma = theta / delta
    rho = 1.0 / sigma
    residual = rhs_in
    direction = residual / theta
    adjoint = direction
    fields = neighbours(direction.astype(jnp.bfloat16))
    coefs = []
    for number in range(ITERS):
        rho_next = 1.0 / (2.0 * sigma - rho)
        coefs.append(jnp.stack([rho_next * rho, 2.0 * rho_next / delta]))
        rho = rho_next

    def first_product(near_parts):
        parts = [packed0, *near_parts, *far(*near_parts)]
        (acc,) = sweep(parts, counts0, codes0, coefs[0], fields)
        return parts, acc

    def with_second(near_parts, packed):
        near1 = near(packed)
        parts, acc = first_product(near_parts)
        return parts, acc, [packed, *near1, *far(*near1)]

    def without_second(near_parts, packed):
        half = packed.shape[0] // 2
        parts, acc = first_product(near_parts)
        return parts, acc, [packed, packed, packed, packed[:half], packed[half:]]

    parts0, acc, parts1 = lax.cond(
        jnp.sum(counts1) > 0, with_second, without_second, near0, packed1
    )
    for number in range(ITERS):
        state = (adjoint, residual, direction)
        final = number + 1 == ITERS
        if number == 0:
            out = sweep(parts1, counts1, codes1, coefs[0], fields, acc, state)
        else:
            out = sweep(
                parts0 + parts1, counts, codes, coefs[number], fields, None, state, final
            )
        if final:
            return out
        rounded, adjoint, residual, direction = out
        fields = neighbours(rounded)


def solution(mesh):
    placed = (
        P(("rows", "rhs"), None, None),
        P(("rows", "rhs"), None, None),
        P(("rows", "rhs"), None),
        P(("rows", "rhs"), None),
        P(("rows", "rhs")),
        P(("rows", "rhs")),
        P(("rows", "rhs")),
        P("rows", "rhs", None),
        P(),
        P(),
    )
    return jax.shard_map(
        local,
        mesh=mesh,
        in_specs=placed,
        out_specs=(P("rows", "rhs", None), P("rows", "rhs", None)),
        check_vma=False,
    )
```

```python
import functools

import jax
import jax.numpy as jnp
from jax import lax
from jax.experimental import pallas as pl
from jax.experimental.pallas import tpu as pltpu
from jax.sharding import PartitionSpec as P

ITERS = 4
CHUNK = 32


def form_kernel(owner, place, left, right, diag, out0, out1, held, sems):
    slots = left.shape[0]
    columns = diag[...].T

    def target(k, out):
        return pltpu.make_async_copy(held.at[k], out.at[owner[k]], sems.at[k])

    for k in range(slots):
        scaled = (columns[:, k : k + 1] * right[k].astype(jnp.float32)).astype(jnp.bfloat16)
        held[k] = jnp.dot(left[k], scaled, preferred_element_type=jnp.float32).astype(jnp.bfloat16)

        @pl.when(place[k] == 0)
        def _():
            target(k, out0).start()

        @pl.when(place[k] != 0)
        def _():
            target(k, out1).start()

    for k in range(slots):
        target(k, out0).wait()


def form_blocks(left, right, diag, owner, place, peers):
    slots, width = diag.shape
    shape = jax.ShapeDtypeStruct((peers, width, width), jnp.bfloat16)
    return pl.pallas_call(
        form_kernel,
        out_shape=(shape, shape),
        grid_spec=pltpu.PrefetchScalarGridSpec(
            num_scalar_prefetch=2,
            in_specs=[pl.BlockSpec(memory_space=pltpu.VMEM)] * 3,
            out_specs=[pl.BlockSpec(memory_space=pltpu.HBM)] * 2,
            scratch_shapes=[
                pltpu.VMEM((slots, width, width), jnp.bfloat16),
                pltpu.SemaphoreType.DMA((slots,)),
            ],
        ),
        name="form_blocks",
    )(owner, place, left, right, diag)


def pack_kernel(order, count, got, packed, sems):
    def begin(j, carry):
        pltpu.make_async_copy(got.at[order[j]], packed.at[j], sems.at[j]).start()
        return carry

    def finish(j, carry):
        pltpu.make_async_copy(got.at[0], packed.at[0], sems.at[j]).wait()
        return carry

    lax.fori_loop(0, count[0], begin, 0)
    lax.fori_loop(0, count[0], finish, 0)


def pack_blocks(got, order, count):
    peers, width, _ = got.shape
    return pl.pallas_call(
        pack_kernel,
        out_shape=jax.ShapeDtypeStruct((peers, width, width), jnp.bfloat16),
        grid_spec=pltpu.PrefetchScalarGridSpec(
            num_scalar_prefetch=2,
            in_specs=[pl.BlockSpec(memory_space=pltpu.VMEM)],
            out_specs=pl.BlockSpec(memory_space=pltpu.HBM),
            scratch_shapes=[pltpu.SemaphoreType.DMA((peers,))],
        ),
        name="pack_blocks",
    )(order, count, got)


def read_bits(rows):
    return (3 * rows - 1).bit_length()


def sweep_kernel(num_parts, half, chunk, has_acc, last, final, *refs):
    counts, codes, coef = refs[:3]
    refs = refs[3:]
    parts, refs = refs[:num_parts], refs[num_parts:]
    fields, refs = refs[:3], refs[3:]
    num_state = 3 * last + has_acc
    state, refs = refs[:num_state], refs[num_state:]
    num_outs = (2 if final else 4) if last else 1
    outs, refs = refs[:num_outs], refs[num_outs:]
    ext, acc, held, kept, rounded, sems, field_sems, state_sems, out_sems = refs
    rows = fields[1].shape[0]
    steps = half // chunk
    halves = [(part, i) for part in parts for i in range(0, part.shape[0], half)]
    bits = read_bits(rows)
    field_copies = [
        pltpu.make_async_copy(field, ext.at[pl.ds(i * rows, rows)], field_sems.at[i])
        for i, field in enumerate(fields)
    ]
    for copy in field_copies:
        copy.start()
    for a, (part, first) in enumerate(halves):
        for c in range(steps):

            @pl.when(counts[a] > c * chunk)
            def _():
                pltpu.make_async_copy(
                    part.at[pl.ds(first + c * chunk, chunk)],
                    held.at[pl.ds(a * half + c * chunk, chunk)],
                    sems.at[a * steps + c],
                ).start()

    used = acc.at[pl.ds(1, rows)]
    state_copies = [
        pltpu.make_async_copy(array, kept.at[i], state_sems.at[i])
        for i, array in enumerate(state[: 3 * last])
    ]
    if has_acc:
        acc_copy = pltpu.make_async_copy(state[-1], used, state_sems.at[3])
        acc_copy.start()
    else:
        used[...] = jnp.zeros(used.shape, jnp.float32)
    acc[0] = jnp.zeros(acc.shape[1:], jnp.float32)
    for copy in state_copies:
        copy.start()
    for copy in field_copies:
        copy.wait()
    if has_acc:
        acc_copy.wait()

    def part_body(a, carry):
        def chunk_body(c, inner):
            base = a * half + c * chunk
            pltpu.make_async_copy(
                parts[0].at[pl.ds(0, chunk)], held.at[pl.ds(base, chunk)], sems.at[a * steps + c]
            ).wait()
            for j in range(chunk):
                code = codes[base + j]
                picked = ext[code & (2**bits - 1)]
                acc[code >> bits] += jnp.dot(
                    picked, held[base + j], preferred_element_type=jnp.float32
                )
            return inner

        return lax.fori_loop(0, lax.div(counts[a] + chunk - 1, chunk), chunk_body, carry)

    lax.fori_loop(0, len(halves), part_body, 0)

    if not last:
        results = [used]
    else:
        for copy in state_copies:
            copy.wait()
        adjoint, residual, direction = (kept.at[i] for i in range(3))
        step = direction[...]
        left = residual[...] - (step - used[...])
        residual[...] = left
        results = [adjoint, residual]
        if not final:
            step = coef[0] * step + coef[1] * left
            rounded[...] = step.astype(jnp.bfloat16)
            direction[...] = step
            adjoint[...] = adjoint[...] + step
            results = [rounded, adjoint, residual, direction]
    out_copies = [
        pltpu.make_async_copy(result, out, out_sems.at[i])
        for i, (result, out) in enumerate(zip(results, outs))
    ]
    for copy in out_copies:
        copy.start()
    for copy in out_copies:
        copy.wait()


def sweep(parts, counts, codes, coef, fields, acc_in=None, state=None, final=False):
    half, width = parts[-1].shape[:2]
    chunk = min(CHUNK, half)
    held = sum(part.shape[0] for part in parts)
    rows, columns, _ = fields[1].shape
    last = state is not None
    wide = jax.ShapeDtypeStruct((rows, columns, width), jnp.float32)
    if not last:
        outs = (wide,)
    elif final:
        outs = (wide, wide)
    else:
        outs = (jax.ShapeDtypeStruct(wide.shape, jnp.bfloat16), wide, wide, wide)
    extra = list(fields) + list(state or ()) + ([acc_in] if acc_in is not None else [])
    return pl.pallas_call(
        functools.partial(sweep_kernel, len(parts), half, chunk, acc_in is not None, last, final),
        out_shape=outs,
        in_specs=[pl.BlockSpec(memory_space=pltpu.SMEM)] * 3
        + [pl.BlockSpec(memory_space=pltpu.HBM)] * (len(parts) + len(extra)),
        out_specs=[pl.BlockSpec(memory_space=pltpu.HBM)] * len(outs),
        scratch_shapes=[
            pltpu.VMEM((3 * rows, columns, width), jnp.bfloat16),
            pltpu.VMEM((rows + 1, columns, width), jnp.float32),
            pltpu.VMEM((held, width, width), jnp.bfloat16),
            pltpu.VMEM((3, rows, columns, width), jnp.float32),
            pltpu.VMEM((rows, columns, width), jnp.bfloat16),
            pltpu.SemaphoreType.DMA((held // chunk,)),
            pltpu.SemaphoreType.DMA((3,)),
            pltpu.SemaphoreType.DMA((4,)),
            pltpu.SemaphoreType.DMA((4,)),
        ],
        compiler_params=pltpu.CompilerParams(vmem_limit_bytes=60 * 2**20),
        name="sweep",
    )(counts, codes, coef, *parts, *extra)


def ring(count, shift):
    return [(i, (i + shift) % count) for i in range(count)]


def near(packed):
    count = lax.axis_size("rhs")
    return (
        lax.ppermute(packed, "rhs", ring(count, 1)),
        lax.ppermute(packed, "rhs", ring(count, -1)),
    )


def far(above, below):
    count = lax.axis_size("rhs")
    half = above.shape[0] // 2
    return (
        lax.ppermute(above[:half], "rhs", ring(count, 1)),
        lax.ppermute(below[half:], "rhs", ring(count, -1)),
    )


def neighbours(rounded):
    count = lax.axis_size("rows")
    return (
        lax.ppermute(rounded, "rows", ring(count, 1)),
        rounded,
        lax.ppermute(rounded, "rows", ring(count, -1)),
    )


def local_program(
    factor_left,
    factor_right,
    state_diag,
    owner,
    col_local,
    row_shift,
    row_local,
    rhs_in,
    low_bound,
    high_bound,
):
    peers = lax.axis_size("rows")
    across = lax.axis_size("rhs")
    slots = owner.shape[0]
    local_rows = rhs_in.shape[0]
    bits = read_bits(local_rows)
    dest = owner[:, 0]
    order = jnp.arange(slots)
    earlier = (dest[:, None] == dest[None, :]) & (order[None, :] < order[:, None])
    place = jnp.sum(earlier.astype(jnp.int32), axis=1)
    code = ((col_local + 1) << bits) + row_shift * local_rows + row_local
    spot = dest * 2 + place
    send_codes = jnp.sum(
        jnp.where(jnp.arange(2 * peers)[:, None] == spot[None, :], code[None, :], 0), axis=1
    )
    got_codes = lax.all_to_all(
        send_codes.reshape(peers, 2), "rows", split_axis=0, concat_axis=0, tiled=True
    ).T
    number = jnp.arange(peers)
    key = jnp.where(got_codes > 0, got_codes, jnp.int32(1 << 20))
    ahead = (key[:, None, :] < key[:, :, None]) | (
        (key[:, None, :] == key[:, :, None]) & (number[None, None, :] < number[None, :, None])
    )
    rank = jnp.sum(ahead.astype(jnp.int32), axis=2)
    chosen = rank[:, None, :] == number[None, :, None]
    source = jnp.sum(jnp.where(chosen, number[None, None, :], 0), axis=2)
    sorted_codes = jnp.sum(jnp.where(chosen, got_codes[:, None, :], 0), axis=2)
    count = jnp.sum((got_codes > 0).astype(jnp.int32), axis=1)

    up = lax.ppermute(sorted_codes, "rhs", ring(across, 1))
    down = lax.ppermute(sorted_codes, "rhs", ring(across, -1))
    far_codes = lax.ppermute(sorted_codes, "rhs", ring(across, 2))
    all_codes = jnp.stack([sorted_codes, up, down, far_codes], axis=1)
    all_codes = all_codes.reshape(2, 4, 2, peers // 2)
    all_counts = jnp.sum((all_codes > 0).astype(jnp.int32), axis=3).reshape(2, 8)
    all_codes = all_codes.reshape(2, 4 * peers)
    low = low_bound[0]
    high = high_bound[0]
    theta = (high + low) / 2.0
    delta = (high - low) / 2.0
    sigma = theta / delta
    rho = 1.0 / sigma
    coefs = []
    for number in range(ITERS):
        rho_next = 1.0 / (2.0 * sigma - rho)
        coefs.append(jnp.stack([rho_next * rho, 2.0 * rho_next / delta]))
        rho = rho_next
    tables = (
        source[1],
        count[1:],
        all_counts[0],
        all_counts[1],
        all_counts.reshape(16),
        all_codes[0],
        all_codes[1],
        all_codes.reshape(8 * peers),
        *coefs,
    )

    sent0, sent1 = form_blocks(factor_left, factor_right, state_diag, dest, place, peers)
    got0 = lax.all_to_all(sent0, "rows", split_axis=0, concat_axis=0, tiled=True)
    packed0 = pack_blocks(got0, source[0], count[:1])
    near0 = near(packed0)
    far0 = far(*near0)
    sent1, _, *tables = lax.optimization_barrier((sent1, packed0, *tables))
    order1, number1, counts0, counts1, counts, codes0, codes1, codes, *coefs = tables
    got1 = lax.all_to_all(sent1, "rows", split_axis=0, concat_axis=0, tiled=True)
    packed1 = pack_blocks(got1, order1, number1)

    residual = rhs_in
    direction = residual / theta
    adjoint = direction
    fields = neighbours(direction.astype(jnp.bfloat16))

    def first_product(parts):
        (acc,) = sweep(parts, counts0, codes0, coefs[0], fields)
        return acc

    def with_second(parts, packed):
        near1 = near(packed)
        acc = first_product(parts)
        return acc, [packed, *near1, *far(*near1)]

    def without_second(parts, packed):
        half = packed.shape[0] // 2
        return first_product(parts), [packed, packed, packed, packed[:half], packed[half:]]

    parts0 = [packed0, *near0, *far0]
    acc, parts1 = lax.cond(jnp.sum(counts1) > 0, with_second, without_second, parts0, packed1)
    for number in range(ITERS):
        state = (adjoint, residual, direction)
        final = number + 1 == ITERS
        if number == 0:
            out = sweep(parts1, counts1, codes1, coefs[0], fields, acc, state)
        else:
            out = sweep(
                parts0 + parts1, counts, codes, coefs[number], fields, None, state, final
            )
        if final:
            return out
        rounded, adjoint, residual, direction = out
        fields = neighbours(rounded)


def solution(mesh):
    placed = (
        P(("rows", "rhs"), None, None),
        P(("rows", "rhs"), None, None),
        P(("rows", "rhs"), None),
        P(("rows", "rhs"), None),
        P(("rows", "rhs")),
        P(("rows", "rhs")),
        P(("rows", "rhs")),
        P("rows", "rhs", None),
        P(),
        P(),
    )
    return jax.shard_map(
        local_program,
        mesh=mesh,
        in_specs=placed,
        out_specs=(P("rows", "rhs", None), P("rows", "rhs", None)),
        check_vma=False,
    )
```

```python
import functools

import jax
import jax.numpy as jnp
from jax import lax
from jax.experimental import pallas as pl
from jax.experimental.pallas import tpu as pltpu
from jax.sharding import PartitionSpec as P

ITERS = 4
CHUNK = 32


def form_kernel(owner, place, left, right, diag, out0, out1, held, sems):
    slots = left.shape[0]
    columns = diag[...].T

    def target(k, out):
        return pltpu.make_async_copy(held.at[k], out.at[owner[k]], sems.at[k])

    for k in range(slots):
        scaled = (columns[:, k : k + 1] * right[k].astype(jnp.float32)).astype(jnp.bfloat16)
        held[k] = jnp.dot(left[k], scaled, preferred_element_type=jnp.float32).astype(jnp.bfloat16)

        @pl.when(place[k] == 0)
        def _():
            target(k, out0).start()

        @pl.when(place[k] != 0)
        def _():
            target(k, out1).start()

    for k in range(slots):
        target(k, out0).wait()


def form_blocks(left, right, diag, owner, place, peers):
    slots, width = diag.shape
    shape = jax.ShapeDtypeStruct((peers, width, width), jnp.bfloat16)
    return pl.pallas_call(
        form_kernel,
        out_shape=(shape, shape),
        grid_spec=pltpu.PrefetchScalarGridSpec(
            num_scalar_prefetch=2,
            in_specs=[pl.BlockSpec(memory_space=pltpu.VMEM)] * 3,
            out_specs=[pl.BlockSpec(memory_space=pltpu.HBM)] * 2,
            scratch_shapes=[
                pltpu.VMEM((slots, width, width), jnp.bfloat16),
                pltpu.SemaphoreType.DMA((slots,)),
            ],
        ),
        name="form_blocks",
    )(owner, place, left, right, diag)


def read_bits(rows):
    return (3 * rows - 1).bit_length()


def sweep_kernel(num_parts, half, chunk, has_acc, last, final, *refs):
    counts, codes, coef = refs[:3]
    refs = refs[3:]
    parts, refs = refs[:num_parts], refs[num_parts:]
    fields, refs = refs[:3], refs[3:]
    num_state = 3 * last + has_acc
    state, refs = refs[:num_state], refs[num_state:]
    num_outs = (2 if final else 4) if last else 1
    outs, refs = refs[:num_outs], refs[num_outs:]
    ext, acc, held, kept, rounded, sems, field_sems, state_sems, out_sems = refs
    rows = fields[1].shape[0]
    steps = half // chunk
    halves = [(part, i) for part in parts for i in range(0, part.shape[0], half)]
    bits = read_bits(rows)
    field_copies = [
        pltpu.make_async_copy(field, ext.at[pl.ds(i * rows, rows)], field_sems.at[i])
        for i, field in enumerate(fields)
    ]
    for copy in field_copies:
        copy.start()
    for a, (part, first) in enumerate(halves):
        for c in range(steps):

            @pl.when(counts[a] > c * chunk)
            def _():
                pltpu.make_async_copy(
                    part.at[pl.ds(first + c * chunk, chunk)],
                    held.at[pl.ds(a * half + c * chunk, chunk)],
                    sems.at[a * steps + c],
                ).start()

    used = acc.at[pl.ds(1, rows)]
    state_copies = [
        pltpu.make_async_copy(array, kept.at[i], state_sems.at[i])
        for i, array in enumerate(state[: 3 * last])
    ]
    if has_acc:
        acc_copy = pltpu.make_async_copy(state[-1], used, state_sems.at[3])
        acc_copy.start()
    else:
        used[...] = jnp.zeros(used.shape, jnp.float32)
    acc[0] = jnp.zeros(acc.shape[1:], jnp.float32)
    for copy in state_copies:
        copy.start()
    for copy in field_copies:
        copy.wait()
    if has_acc:
        acc_copy.wait()

    def part_body(a, carry):
        def chunk_body(c, inner):
            base = a * half + c * chunk
            pltpu.make_async_copy(
                parts[0].at[pl.ds(0, chunk)], held.at[pl.ds(base, chunk)], sems.at[a * steps + c]
            ).wait()
            for j in range(chunk):
                code = codes[base + j]
                picked = ext[code & (2**bits - 1)]
                acc[code >> bits] += jnp.dot(
                    picked, held[base + j], preferred_element_type=jnp.float32
                )
            return inner

        return lax.fori_loop(0, lax.div(counts[a] + chunk - 1, chunk), chunk_body, carry)

    lax.fori_loop(0, len(halves), part_body, 0)

    if not last:
        results = [used]
    else:
        for copy in state_copies:
            copy.wait()
        adjoint, residual, direction = (kept.at[i] for i in range(3))
        step = direction[...]
        left = residual[...] - (step - used[...])
        residual[...] = left
        results = [adjoint, residual]
        if not final:
            step = coef[0] * step + coef[1] * left
            rounded[...] = step.astype(jnp.bfloat16)
            direction[...] = step
            adjoint[...] = adjoint[...] + step
            results = [rounded, adjoint, residual, direction]
    out_copies = [
        pltpu.make_async_copy(result, out, out_sems.at[i])
        for i, (result, out) in enumerate(zip(results, outs))
    ]
    for copy in out_copies:
        copy.start()
    for copy in out_copies:
        copy.wait()


def sweep(parts, counts, codes, coef, fields, acc_in=None, state=None, final=False):
    half, width = min(part.shape[0] for part in parts), parts[0].shape[1]
    chunk = min(CHUNK, half)
    held = sum(part.shape[0] for part in parts)
    rows, columns, _ = fields[1].shape
    last = state is not None
    wide = jax.ShapeDtypeStruct((rows, columns, width), jnp.float32)
    if not last:
        outs = (wide,)
    elif final:
        outs = (wide, wide)
    else:
        outs = (jax.ShapeDtypeStruct(wide.shape, jnp.bfloat16), wide, wide, wide)
    extra = list(fields) + list(state or ()) + ([acc_in] if acc_in is not None else [])
    return pl.pallas_call(
        functools.partial(sweep_kernel, len(parts), half, chunk, acc_in is not None, last, final),
        out_shape=outs,
        in_specs=[pl.BlockSpec(memory_space=pltpu.SMEM)] * 3
        + [pl.BlockSpec(memory_space=pltpu.HBM)] * (len(parts) + len(extra)),
        out_specs=[pl.BlockSpec(memory_space=pltpu.HBM)] * len(outs),
        scratch_shapes=[
            pltpu.VMEM((3 * rows, columns, width), jnp.bfloat16),
            pltpu.VMEM((rows + 1, columns, width), jnp.float32),
            pltpu.VMEM((held, width, width), jnp.bfloat16),
            pltpu.VMEM((3, rows, columns, width), jnp.float32),
            pltpu.VMEM((rows, columns, width), jnp.bfloat16),
            pltpu.SemaphoreType.DMA((held // chunk,)),
            pltpu.SemaphoreType.DMA((3,)),
            pltpu.SemaphoreType.DMA((4,)),
            pltpu.SemaphoreType.DMA((4,)),
        ],
        compiler_params=pltpu.CompilerParams(vmem_limit_bytes=60 * 2**20),
        name="sweep",
    )(counts, codes, coef, *parts, *extra)


def ring(count, shift):
    return [(i, (i + shift) % count) for i in range(count)]


def near(packed):
    count = lax.axis_size("rhs")
    return (
        lax.ppermute(packed, "rhs", ring(count, 1)),
        lax.ppermute(packed, "rhs", ring(count, -1)),
    )


def far(above, below):
    count = lax.axis_size("rhs")
    return (
        lax.ppermute(above, "rhs", ring(count, 1)),
        lax.ppermute(below, "rhs", ring(count, -1)),
    )


def neighbours(rounded):
    count = lax.axis_size("rows")
    return (
        lax.ppermute(rounded, "rows", ring(count, 1)),
        rounded,
        lax.ppermute(rounded, "rows", ring(count, -1)),
    )


def local_program(
    factor_left,
    factor_right,
    state_diag,
    owner,
    col_local,
    row_shift,
    row_local,
    rhs_in,
    low_bound,
    high_bound,
):
    peers = lax.axis_size("rows")
    across = lax.axis_size("rhs")
    slots = owner.shape[0]
    local_rows = rhs_in.shape[0]
    bits = read_bits(local_rows)
    dest = owner[:, 0]
    order = jnp.arange(slots)
    earlier = (dest[:, None] == dest[None, :]) & (order[None, :] < order[:, None])
    place = jnp.sum(earlier.astype(jnp.int32), axis=1)
    code = ((col_local + 1) << bits) + row_shift * local_rows + row_local
    spot = dest * 2 + place
    send_codes = jnp.sum(
        jnp.where(jnp.arange(2 * peers)[:, None] == spot[None, :], code[None, :], 0), axis=1
    )
    sent0, sent1 = form_blocks(factor_left, factor_right, state_diag, dest, place, peers)
    got0 = lax.all_to_all(sent0, "rows", split_axis=0, concat_axis=0, tiled=True)
    near0 = near(got0)
    half = peers // 2
    far0 = far(near0[0][:half], near0[1][half:])
    send_codes, _ = lax.optimization_barrier((send_codes, got0))
    got_codes = lax.all_to_all(
        send_codes.reshape(peers, 2), "rows", split_axis=0, concat_axis=0, tiled=True
    ).T
    sent1, got_codes = lax.optimization_barrier((sent1, got_codes))
    got1 = lax.all_to_all(sent1, "rows", split_axis=0, concat_axis=0, tiled=True)

    up = lax.ppermute(got_codes, "rhs", ring(across, 1))
    down = lax.ppermute(got_codes, "rhs", ring(across, -1))
    far_codes = lax.ppermute(got_codes, "rhs", ring(across, 2))
    all_codes = jnp.stack([got_codes, up, down, far_codes], axis=1)
    all_codes = all_codes.reshape(2, 4, 2, half)
    all_counts = half * jnp.any(all_codes > 0, axis=3).astype(jnp.int32).reshape(2, 8)
    all_codes = all_codes.reshape(2, 4 * peers)

    low = low_bound[0]
    high = high_bound[0]
    theta = (high + low) / 2.0
    delta = (high - low) / 2.0
    sigma = theta / delta
    rho = 1.0 / sigma
    coefs = []
    for _ in range(ITERS):
        rho_next = 1.0 / (2.0 * sigma - rho)
        coefs.append(jnp.stack([rho_next * rho, 2.0 * rho_next / delta]))
        rho = rho_next
    tables = (
        all_counts[0],
        all_counts[1],
        all_counts.reshape(16),
        all_codes[0],
        all_codes[1],
        all_codes.reshape(8 * peers),
        *coefs,
    )

    got1, *tables = lax.optimization_barrier((got1, *tables))
    counts0, counts1, counts, codes0, codes1, codes, *coefs = tables

    residual = rhs_in
    direction = residual / theta
    adjoint = direction
    fields = neighbours(direction.astype(jnp.bfloat16))

    def first_product(parts):
        (acc,) = sweep(parts, counts0, codes0, coefs[0], fields)
        return acc

    def with_second(parts, got):
        first, second = got[:half], got[half:]
        up_first = lax.ppermute(first, "rhs", ring(across, 1))
        down_second = lax.ppermute(second, "rhs", ring(across, -1))
        up_second = lax.ppermute(second, "rhs", ring(across, 1))
        down_first = lax.ppermute(first, "rhs", ring(across, -1))
        acc = first_product(parts)
        far1 = far(up_first, down_second)
        return acc, [up_first, up_second, down_first, down_second, *far1]

    def without_second(parts, got):
        return first_product(parts), [jnp.zeros(got[:half].shape, got.dtype)] * 6

    parts0 = [got0, *near0, *far0]
    acc, others1 = lax.cond(jnp.sum(counts1) > 0, with_second, without_second, parts0, got1)
    parts1 = [got1, *others1]
    for number in range(ITERS):
        state = (adjoint, residual, direction)
        final = number + 1 == ITERS
        if number == 0:
            out = sweep(parts1, counts1, codes1, coefs[0], fields, acc, state)
        else:
            out = sweep(
                parts0 + parts1, counts, codes, coefs[number], fields, None, state, final
            )
        if final:
            return out
        rounded, adjoint, residual, direction = out
        fields = neighbours(rounded)


def solution(mesh):
    placed = (
        P(("rows", "rhs"), None, None),
        P(("rows", "rhs"), None, None),
        P(("rows", "rhs"), None),
        P(("rows", "rhs"), None),
        P(("rows", "rhs")),
        P(("rows", "rhs")),
        P(("rows", "rhs")),
        P("rows", "rhs", None),
        P(),
        P(),
    )
    return jax.shard_map(
        local_program,
        mesh=mesh,
        in_specs=placed,
        out_specs=(P("rows", "rhs", None), P("rows", "rhs", None)),
        check_vma=False,
    )
```

```python
import functools

import jax
import jax.numpy as jnp
from jax import lax
from jax.experimental import pallas as pl
from jax.experimental.pallas import tpu as pltpu
from jax.sharding import PartitionSpec as P

ITERS = 4


def form_kernel(owner, place, left, right, diag, out0, out1, held, sems):
    slots = left.shape[0]
    columns = diag[...].T

    def target(k, out):
        return pltpu.make_async_copy(held.at[k], out.at[owner[k]], sems.at[k])

    for k in range(slots):
        scaled = (columns[:, k : k + 1] * right[k].astype(jnp.float32)).astype(jnp.bfloat16)
        held[k] = jnp.dot(left[k], scaled, preferred_element_type=jnp.float32).astype(jnp.bfloat16)

        @pl.when(place[k] == 0)
        def _():
            target(k, out0).start()

        @pl.when(place[k] != 0)
        def _():
            target(k, out1).start()

    for k in range(slots):
        target(k, out0).wait()


def form_blocks(left, right, diag, owner, place, peers):
    slots, width = diag.shape
    shape = jax.ShapeDtypeStruct((peers, width, width), jnp.bfloat16)
    return pl.pallas_call(
        form_kernel,
        out_shape=(shape, shape),
        grid_spec=pltpu.PrefetchScalarGridSpec(
            num_scalar_prefetch=2,
            in_specs=[pl.BlockSpec(memory_space=pltpu.VMEM)] * 3,
            out_specs=[pl.BlockSpec(memory_space=pltpu.HBM)] * 2,
            scratch_shapes=[
                pltpu.VMEM((slots, width, width), jnp.bfloat16),
                pltpu.SemaphoreType.DMA((slots,)),
            ],
        ),
        name="form_blocks",
    )(owner, place, left, right, diag)


def read_bits(rows):
    return (3 * rows - 1).bit_length()


def sweep_kernel(num_parts, half, has_acc, last, final, *refs):
    counts, codes, coef = refs[:3]
    refs = refs[3:]
    parts, refs = refs[:num_parts], refs[num_parts:]
    fields, refs = refs[:3], refs[3:]
    num_state = 3 * last + has_acc
    state, refs = refs[:num_state], refs[num_state:]
    num_outs = (2 if final else 4) if last else 1
    outs, refs = refs[:num_outs], refs[num_outs:]
    ext, acc, held, kept, rounded, sems, field_sems, state_sems, out_sems = refs
    rows = fields[1].shape[0]
    group = 2 * half
    halves = [(part, i) for part in parts for i in range(0, part.shape[0], half)]
    bits = read_bits(rows)
    field_copies = [
        pltpu.make_async_copy(field, ext.at[pl.ds(i * rows, rows)], field_sems.at[i])
        for i, field in enumerate(fields)
    ]
    for copy in field_copies:
        copy.start()
    for a, (part, first) in enumerate(halves):

        @pl.when(counts[a // 2] > 0)
        def _():
            pltpu.make_async_copy(
                part.at[pl.ds(first, half)], held.at[pl.ds(a * half, half)], sems.at[a]
            ).start()

    used = acc.at[pl.ds(1, rows)]
    state_copies = [
        pltpu.make_async_copy(array, kept.at[i], state_sems.at[i])
        for i, array in enumerate(state[: 3 * last])
    ]
    if has_acc:
        acc_copy = pltpu.make_async_copy(state[-1], used, state_sems.at[3])
        acc_copy.start()
    else:
        used[...] = jnp.zeros(used.shape, jnp.float32)
    acc[0] = jnp.zeros(acc.shape[1:], jnp.float32)
    for copy in state_copies:
        copy.start()
    for copy in field_copies:
        copy.wait()
    if has_acc:
        acc_copy.wait()

    def group_body(g, carry):
        base = g * group

        @pl.when(counts[g] > 0)
        def _():
            for i in range(2):
                pltpu.make_async_copy(
                    parts[-1], held.at[pl.ds(base + i * half, half)], sems.at[2 * g + i]
                ).wait()
            for j in range(group):
                code = codes[base + j]
                picked = ext[code & (2**bits - 1)]
                acc[code >> bits] += jnp.dot(
                    picked, held[base + j], preferred_element_type=jnp.float32
                )

        return carry

    lax.fori_loop(0, len(halves) // 2, group_body, 0)

    if not last:
        results = [used]
    else:
        for copy in state_copies:
            copy.wait()
        adjoint, residual, direction = (kept.at[i] for i in range(3))
        step = direction[...]
        left = residual[...] - (step - used[...])
        residual[...] = left
        results = [adjoint, residual]
        if not final:
            step = coef[0] * step + coef[1] * left
            rounded[...] = step.astype(jnp.bfloat16)
            direction[...] = step
            adjoint[...] = adjoint[...] + step
            results = [rounded, adjoint, residual, direction]
    out_copies = [
        pltpu.make_async_copy(result, out, out_sems.at[i])
        for i, (result, out) in enumerate(zip(results, outs))
    ]
    for copy in out_copies:
        copy.start()
    for copy in out_copies:
        copy.wait()


def sweep(parts, counts, codes, coef, fields, acc_in=None, state=None, final=False):
    half, width = min(part.shape[0] for part in parts), parts[0].shape[1]
    held = sum(part.shape[0] for part in parts)
    rows, columns, _ = fields[1].shape
    last = state is not None
    wide = jax.ShapeDtypeStruct((rows, columns, width), jnp.float32)
    if not last:
        outs = (wide,)
    elif final:
        outs = (wide, wide)
    else:
        outs = (jax.ShapeDtypeStruct(wide.shape, jnp.bfloat16), wide, wide, wide)
    extra = list(fields) + list(state or ()) + ([acc_in] if acc_in is not None else [])
    return pl.pallas_call(
        functools.partial(sweep_kernel, len(parts), half, acc_in is not None, last, final),
        out_shape=outs,
        in_specs=[pl.BlockSpec(memory_space=pltpu.SMEM)] * 3
        + [pl.BlockSpec(memory_space=pltpu.HBM)] * (len(parts) + len(extra)),
        out_specs=[pl.BlockSpec(memory_space=pltpu.HBM)] * len(outs),
        scratch_shapes=[
            pltpu.VMEM((3 * rows, columns, width), jnp.bfloat16),
            pltpu.VMEM((rows + 1, columns, width), jnp.float32),
            pltpu.VMEM((held, width, width), jnp.bfloat16),
            pltpu.VMEM((3, rows, columns, width), jnp.float32),
            pltpu.VMEM((rows, columns, width), jnp.bfloat16),
            pltpu.SemaphoreType.DMA((held // half,)),
            pltpu.SemaphoreType.DMA((3,)),
            pltpu.SemaphoreType.DMA((4,)),
            pltpu.SemaphoreType.DMA((4,)),
        ],
        compiler_params=pltpu.CompilerParams(vmem_limit_bytes=60 * 2**20),
        name="sweep",
    )(counts, codes, coef, *parts, *extra)


def ring(count, shift):
    return [(i, (i + shift) % count) for i in range(count)]


def near(packed):
    count = lax.axis_size("rhs")
    return (
        lax.ppermute(packed, "rhs", ring(count, 1)),
        lax.ppermute(packed, "rhs", ring(count, -1)),
    )


def far(above, below):
    count = lax.axis_size("rhs")
    return (
        lax.ppermute(above, "rhs", ring(count, 1)),
        lax.ppermute(below, "rhs", ring(count, -1)),
    )


def neighbours(rounded):
    count = lax.axis_size("rows")
    return (
        lax.ppermute(rounded, "rows", ring(count, 1)),
        rounded,
        lax.ppermute(rounded, "rows", ring(count, -1)),
    )


def local_program(
    factor_left,
    factor_right,
    state_diag,
    owner,
    col_local,
    row_shift,
    row_local,
    rhs_in,
    low_bound,
    high_bound,
):
    peers = lax.axis_size("rows")
    across = lax.axis_size("rhs")
    slots = owner.shape[0]
    local_rows = rhs_in.shape[0]
    bits = read_bits(local_rows)
    dest = owner[:, 0]
    order = jnp.arange(slots)
    earlier = (dest[:, None] == dest[None, :]) & (order[None, :] < order[:, None])
    place = jnp.sum(earlier.astype(jnp.int32), axis=1)
    code = ((col_local + 1) << bits) + row_shift * local_rows + row_local
    spot = dest * 2 + place
    send_codes = jnp.sum(
        jnp.where(jnp.arange(2 * peers)[:, None] == spot[None, :], code[None, :], 0), axis=1
    )
    sent0, sent1 = form_blocks(factor_left, factor_right, state_diag, dest, place, peers)
    got0 = lax.all_to_all(sent0, "rows", split_axis=0, concat_axis=0, tiled=True)
    near0 = near(got0)
    half = peers // 2
    far0 = far(near0[0][:half], near0[1][half:])
    send_codes, _ = lax.optimization_barrier((send_codes, got0))
    got_codes = lax.all_to_all(
        send_codes.reshape(peers, 2), "rows", split_axis=0, concat_axis=0, tiled=True
    ).T
    sent1, got_codes = lax.optimization_barrier((sent1, got_codes))
    got1 = lax.all_to_all(sent1, "rows", split_axis=0, concat_axis=0, tiled=True)

    up = lax.ppermute(got_codes, "rhs", ring(across, 1))
    down = lax.ppermute(got_codes, "rhs", ring(across, -1))
    far_codes = lax.ppermute(got_codes, "rhs", ring(across, 2))
    all_codes = jnp.stack([got_codes, up, down, far_codes], axis=1)
    all_codes = all_codes.reshape(2, 4, 2, half)
    all_counts = jnp.any(all_codes > 0, axis=(2, 3)).astype(jnp.int32)
    all_codes = all_codes.reshape(2, 4 * peers)

    low = low_bound[0]
    high = high_bound[0]
    theta = (high + low) / 2.0
    delta = (high - low) / 2.0
    sigma = theta / delta
    rho = 1.0 / sigma
    coefs = []
    for _ in range(ITERS):
        rho_next = 1.0 / (2.0 * sigma - rho)
        coefs.append(jnp.stack([rho_next * rho, 2.0 * rho_next / delta]))
        rho = rho_next
    tables = (
        all_counts[0],
        all_counts[1],
        all_counts.reshape(8),
        all_counts[1, 3:],
        all_codes[1, 3 * peers :],
        all_codes[0],
        all_codes[1],
        all_codes.reshape(8 * peers),
        *coefs,
    )

    got1, *tables = lax.optimization_barrier((got1, *tables))
    counts0, counts1, counts, counts2, codes2, codes0, codes1, codes, *coefs = tables

    residual = rhs_in
    direction = residual / theta
    adjoint = direction
    fields = neighbours(direction.astype(jnp.bfloat16))

    def with_second(parts, first, second):
        up_first = lax.ppermute(first, "rhs", ring(across, 1))
        down_second = lax.ppermute(second, "rhs", ring(across, -1))
        up_second = lax.ppermute(second, "rhs", ring(across, 1))
        down_first = lax.ppermute(first, "rhs", ring(across, -1))
        near1 = [first, second, up_first, up_second, down_first, down_second]
        far1 = far(up_first, down_second)
        (acc,) = sweep(parts, counts0, codes0, coefs[0], fields)
        (acc,) = sweep(near1, counts1, codes1, coefs[0], fields, acc)
        return acc, near1[2:], list(far1)

    def without_second(parts, first, second):
        (acc,) = sweep(parts, counts0, codes0, coefs[0], fields)
        blank = jnp.zeros(first.shape, first.dtype)
        return acc, [blank] * 4, [blank] * 2

    parts0 = [got0, *near0, *far0]
    local1 = [got1[:half], got1[half:]]
    acc, others1, far1 = lax.cond(
        jnp.sum(counts1) > 0, with_second, without_second, parts0, *local1
    )
    parts1 = [*local1, *others1, *far1]
    for number in range(ITERS):
        state = (adjoint, residual, direction)
        final = number + 1 == ITERS
        if number == 0:
            out = sweep(far1, counts2, codes2, coefs[0], fields, acc, state)
        else:
            out = sweep(
                parts0 + parts1, counts, codes, coefs[number], fields, None, state, final
            )
        if final:
            return out
        rounded, adjoint, residual, direction = out
        fields = neighbours(rounded)


def solution(mesh):
    placed = (
        P(("rows", "rhs"), None, None),
        P(("rows", "rhs"), None, None),
        P(("rows", "rhs"), None),
        P(("rows", "rhs"), None),
        P(("rows", "rhs")),
        P(("rows", "rhs")),
        P(("rows", "rhs")),
        P("rows", "rhs", None),
        P(),
        P(),
    )
    return jax.shard_map(
        local_program,
        mesh=mesh,
        in_specs=placed,
        out_specs=(P("rows", "rhs", None), P("rows", "rhs", None)),
        check_vma=False,
    )
```

```python
import functools

import jax
import jax.numpy as jnp
from jax import lax
from jax.experimental import pallas as pl
from jax.experimental.pallas import tpu as pltpu
from jax.sharding import PartitionSpec as P

ITERS = 4


def form_kernel(owner, place, left, right, diag, out0, out1, held, sems):
    slots = left.shape[0]
    columns = diag[...].T

    def target(k, out):
        return pltpu.make_async_copy(held.at[k], out.at[owner[k]], sems.at[k])

    for k in range(slots):
        scaled = (columns[:, k : k + 1] * right[k].astype(jnp.float32)).astype(jnp.bfloat16)
        held[k] = jnp.dot(left[k], scaled, preferred_element_type=jnp.float32).astype(jnp.bfloat16)

        @pl.when(place[k] == 0)
        def _():
            target(k, out0).start()

        @pl.when(place[k] != 0)
        def _():
            target(k, out1).start()

    for k in range(slots):
        target(k, out0).wait()


def form_blocks(left, right, diag, owner, place, peers):
    slots, width = diag.shape
    shape = jax.ShapeDtypeStruct((peers, width, width), jnp.bfloat16)
    return pl.pallas_call(
        form_kernel,
        out_shape=(shape, shape),
        grid_spec=pltpu.PrefetchScalarGridSpec(
            num_scalar_prefetch=2,
            in_specs=[pl.BlockSpec(memory_space=pltpu.VMEM)] * 3,
            out_specs=[pl.BlockSpec(memory_space=pltpu.HBM)] * 2,
            scratch_shapes=[
                pltpu.VMEM((slots, width, width), jnp.bfloat16),
                pltpu.SemaphoreType.DMA((slots,)),
            ],
        ),
        name="form_blocks",
    )(owner, place, left, right, diag)


def read_bits(rows):
    return (3 * rows - 1).bit_length()


def sweep_kernel(num_parts, half, has_acc, last, final, *refs):
    counts, codes, coef = refs[:3]
    refs = refs[3:]
    parts, refs = refs[:num_parts], refs[num_parts:]
    fields, refs = refs[:3], refs[3:]
    num_state = (2 if final else 3 * last) + has_acc
    state, refs = refs[:num_state], refs[num_state:]
    num_outs = 4 if last and not final else 1
    outs, refs = refs[:num_outs], refs[num_outs:]
    ext, acc, held, kept, rounded, sems, field_sems, state_sems, out_sems = refs
    rows = fields[1].shape[0]
    group = 2 * half
    halves = [(part, i) for part in parts for i in range(0, part.shape[0], half)]
    bits = read_bits(rows)
    field_copies = [
        pltpu.make_async_copy(field, ext.at[pl.ds(i * rows, rows)], field_sems.at[i])
        for i, field in enumerate(fields)
    ]
    for copy in field_copies:
        copy.start()
    for a, (part, first) in enumerate(halves):

        @pl.when(counts[a // 2] > 0)
        def _():
            pltpu.make_async_copy(
                part.at[pl.ds(first, half)], held.at[pl.ds(a * half, half)], sems.at[a]
            ).start()

    used = acc.at[pl.ds(1, rows)]
    state_copies = [
        pltpu.make_async_copy(array, kept.at[i], state_sems.at[i])
        for i, array in enumerate(state[: num_state - has_acc])
    ]
    if has_acc:
        acc_copy = pltpu.make_async_copy(state[-1], used, state_sems.at[3])
        acc_copy.start()
    else:
        used[...] = jnp.zeros(used.shape, jnp.float32)
    acc[0] = jnp.zeros(acc.shape[1:], jnp.float32)
    for copy in state_copies:
        copy.start()
    for copy in field_copies:
        copy.wait()
    if has_acc:
        acc_copy.wait()

    def group_body(g, carry):
        base = g * group

        @pl.when(counts[g] > 0)
        def _():
            for i in range(2):
                pltpu.make_async_copy(
                    parts[-1], held.at[pl.ds(base + i * half, half)], sems.at[2 * g + i]
                ).wait()
            for j in range(group):
                code = codes[base + j]
                picked = ext[code & (2**bits - 1)]
                acc[code >> bits] += jnp.dot(
                    picked, held[base + j], preferred_element_type=jnp.float32
                )

        return carry

    lax.fori_loop(0, len(halves) // 2, group_body, 0)

    if not last:
        results = [used]
    else:
        for copy in state_copies:
            copy.wait()
        residual, direction, adjoint = (kept.at[i] for i in range(3))
        step = direction[...]
        left = residual[...] - (step - used[...])
        residual[...] = left
        results = [residual]
        if not final:
            step = coef[0] * step + coef[1] * left
            rounded[...] = step.astype(jnp.bfloat16)
            direction[...] = step
            adjoint[...] = adjoint[...] + step
            results = [rounded, adjoint, residual, direction]
    out_copies = [
        pltpu.make_async_copy(result, out, out_sems.at[i])
        for i, (result, out) in enumerate(zip(results, outs))
    ]
    for copy in out_copies:
        copy.start()
    for copy in out_copies:
        copy.wait()


def sweep(parts, counts, codes, coef, fields, acc_in=None, state=None, final=False):
    half, width = min(part.shape[0] for part in parts), parts[0].shape[1]
    held = sum(part.shape[0] for part in parts)
    rows, columns, _ = fields[1].shape
    last = state is not None
    wide = jax.ShapeDtypeStruct((rows, columns, width), jnp.float32)
    if not last:
        outs = (wide,)
    elif final:
        outs = (wide,)
    else:
        outs = (jax.ShapeDtypeStruct(wide.shape, jnp.bfloat16), wide, wide, wide)
    extra = list(fields) + list(state or ()) + ([acc_in] if acc_in is not None else [])
    return pl.pallas_call(
        functools.partial(sweep_kernel, len(parts), half, acc_in is not None, last, final),
        out_shape=outs,
        in_specs=[pl.BlockSpec(memory_space=pltpu.SMEM)] * 3
        + [pl.BlockSpec(memory_space=pltpu.HBM)] * (len(parts) + len(extra)),
        out_specs=[pl.BlockSpec(memory_space=pltpu.HBM)] * len(outs),
        scratch_shapes=[
            pltpu.VMEM((3 * rows, columns, width), jnp.bfloat16),
            pltpu.VMEM((rows + 1, columns, width), jnp.float32),
            pltpu.VMEM((held, width, width), jnp.bfloat16),
            pltpu.VMEM((3, rows, columns, width), jnp.float32),
            pltpu.VMEM((rows, columns, width), jnp.bfloat16),
            pltpu.SemaphoreType.DMA((held // half,)),
            pltpu.SemaphoreType.DMA((3,)),
            pltpu.SemaphoreType.DMA((4,)),
            pltpu.SemaphoreType.DMA((4,)),
        ],
        compiler_params=pltpu.CompilerParams(vmem_limit_bytes=48 * 2**20),
        name="sweep",
    )(counts, codes, coef, *parts, *extra)


def ring(count, shift):
    return [(i, (i + shift) % count) for i in range(count)]


def near(packed):
    count = lax.axis_size("rhs")
    return (
        lax.ppermute(packed, "rhs", ring(count, 1)),
        lax.ppermute(packed, "rhs", ring(count, -1)),
    )


def far(above, below):
    count = lax.axis_size("rhs")
    return (
        lax.ppermute(above, "rhs", ring(count, 1)),
        lax.ppermute(below, "rhs", ring(count, -1)),
    )


def neighbours(rounded):
    count = lax.axis_size("rows")
    return (
        lax.ppermute(rounded, "rows", ring(count, 1)),
        rounded,
        lax.ppermute(rounded, "rows", ring(count, -1)),
    )


def local_program(
    factor_left,
    factor_right,
    state_diag,
    owner,
    col_local,
    row_shift,
    row_local,
    rhs_in,
    low_bound,
    high_bound,
):
    peers = lax.axis_size("rows")
    across = lax.axis_size("rhs")
    slots = owner.shape[0]
    local_rows = rhs_in.shape[0]
    bits = read_bits(local_rows)
    dest = owner[:, 0]
    order = jnp.arange(slots)
    earlier = (dest[:, None] == dest[None, :]) & (order[None, :] < order[:, None])
    place = jnp.sum(earlier.astype(jnp.int32), axis=1)
    code = ((col_local + 1) << bits) + row_shift * local_rows + row_local
    spot = dest * 2 + place
    send_codes = jnp.sum(
        jnp.where(jnp.arange(2 * peers)[:, None] == spot[None, :], code[None, :], 0), axis=1
    )
    sent0, sent1 = form_blocks(factor_left, factor_right, state_diag, dest, place, peers)
    got0 = lax.all_to_all(sent0, "rows", split_axis=0, concat_axis=0, tiled=True)
    near0 = near(got0)
    half = peers // 2
    far0 = far(near0[0][:half], near0[1][half:])
    send_codes, _ = lax.optimization_barrier((send_codes, got0))
    got_codes = lax.all_to_all(
        send_codes.reshape(peers, 2), "rows", split_axis=0, concat_axis=0, tiled=True
    ).T
    sent1, got_codes = lax.optimization_barrier((sent1, got_codes))
    got1 = lax.all_to_all(sent1, "rows", split_axis=0, concat_axis=0, tiled=True)

    up = lax.ppermute(got_codes, "rhs", ring(across, 1))
    down = lax.ppermute(got_codes, "rhs", ring(across, -1))
    far_codes = lax.ppermute(got_codes, "rhs", ring(across, 2))
    all_codes = jnp.stack([got_codes, up, down, far_codes], axis=1)
    all_codes = all_codes.reshape(2, 4, 2, half)
    all_counts = jnp.any(all_codes > 0, axis=(2, 3)).astype(jnp.int32)
    all_codes = all_codes.reshape(2, 4 * peers)

    low = low_bound[0]
    high = high_bound[0]
    theta = (high + low) / 2.0
    delta = (high - low) / 2.0
    sigma = theta / delta
    rho = 1.0 / sigma
    coefs = []
    for _ in range(ITERS):
        rho_next = 1.0 / (2.0 * sigma - rho)
        coefs.append(jnp.stack([rho_next * rho, 2.0 * rho_next / delta]))
        rho = rho_next
    tables = (
        all_counts[0],
        all_counts[1],
        all_counts.reshape(8),
        all_counts[1, 3:],
        all_codes[1, 3 * peers :],
        all_codes[0],
        all_codes[1],
        all_codes.reshape(8 * peers),
        *coefs,
    )

    got1, *tables = lax.optimization_barrier((got1, *tables))
    counts0, counts1, counts, counts2, codes2, codes0, codes1, codes, *coefs = tables

    residual = rhs_in
    direction = residual / theta
    adjoint = direction
    fields = neighbours(direction.astype(jnp.bfloat16))

    def with_second(parts, first, second):
        up_first = lax.ppermute(first, "rhs", ring(across, 1))
        down_second = lax.ppermute(second, "rhs", ring(across, -1))
        up_second = lax.ppermute(second, "rhs", ring(across, 1))
        down_first = lax.ppermute(first, "rhs", ring(across, -1))
        near1 = [first, second, up_first, up_second, down_first, down_second]
        far1 = far(up_first, down_second)
        (acc,) = sweep(parts, counts0, codes0, coefs[0], fields)
        (acc,) = sweep(near1, counts1, codes1, coefs[0], fields, acc)
        return acc, near1[2:], list(far1)

    def without_second(parts, first, second):
        (acc,) = sweep(parts, counts0, codes0, coefs[0], fields)
        blank = jnp.zeros(first.shape, first.dtype)
        return acc, [blank] * 4, [blank] * 2

    parts0 = [got0, *near0, *far0]
    local1 = [got1[:half], got1[half:]]
    acc, others1, far1 = lax.cond(
        jnp.sum(counts1) > 0, with_second, without_second, parts0, *local1
    )
    parts1 = [*local1, *others1, *far1]
    for number in range(ITERS):
        final = number + 1 == ITERS
        state = (residual, direction) if final else (residual, direction, adjoint)
        if number == 0:
            out = sweep(far1, counts2, codes2, coefs[0], fields, acc, state)
        else:
            out = sweep(
                parts0 + parts1, counts, codes, coefs[number], fields, None, state, final
            )
        if final:
            return adjoint, out[0]
        rounded, adjoint, residual, direction = out
        fields = neighbours(rounded)


def solution(mesh):
    placed = (
        P(("rows", "rhs"), None, None),
        P(("rows", "rhs"), None, None),
        P(("rows", "rhs"), None),
        P(("rows", "rhs"), None),
        P(("rows", "rhs")),
        P(("rows", "rhs")),
        P(("rows", "rhs")),
        P("rows", "rhs", None),
        P(),
        P(),
    )
    return jax.shard_map(
        local_program,
        mesh=mesh,
        in_specs=placed,
        out_specs=(P("rows", "rhs", None), P("rows", "rhs", None)),
        check_vma=False,
    )
```
